256 devices in a mesh: blk: 32 (over y_lo, z, core), grp: 8 (over y_hi, x).
Axes of the slice: x: 4, y: 4 (y_hi: 2, y_lo: 2; y = y_hi * 2 + y_lo), z: 8, core: 2. Of those that a mesh axis runs over, the one named last changes fastest.
Arguments:
- orbitals: float32 [16384, 512], P('blk'), may hold values from -6 to 6
- points: float32 [3, 16384], P(None, 'blk'), may hold values from 0 to 1
Outputs:
- exchange_vectors: float32 [16384, 512], P('blk')
The draws below stay inside these ranges and needn't reach their ends.
All inputs are finite; a program needn't handle non-finite values.
Results may differ from the reference program's by a relative error of at most 0.0003.
Values sent between devices are 32-bit elements; how exact they have to be, the bound alone decides.
No kernel may reach another device: no remote copies, remote signals or barrier semaphores. Data moves between devices by JAX's collectives and lax.ppermute only.
A program may use at most 64 MiB of HBM per device.

```python
import jax
import jax.numpy as jnp
from jax import lax

PTS_DEV = 512
NORB = 512
POINTS = 16384
N_BLK = 32


def shard_levels(key, shape, shards, least, largest):
    level, own = 1.0, jax.random.fold_in(key, 6)
    for dim, parts in shards:
        steps = jnp.exp(jax.random.uniform(jax.random.fold_in(own, dim), (parts,), jnp.float32, least / len(shards), largest / len(shards)))
        level = level * jnp.repeat(steps, shape[dim] // parts).reshape([-1 if axis == dim else 1 for axis in range(len(shape))])
    return level


def normal_values(key, extent, deviation, reach, shards=(), kind=jnp.bfloat16):
    gain = shard_levels(key, extent, shards, -0.22, 0.18) if shards else 1.0
    result = jax.random.normal(key, extent, jnp.float32) * deviation * gain
    return jnp.minimum(jnp.maximum(result, -reach), reach).astype(kind)


def setup_inputs(seed: int = 0) -> dict:
    streams_of = jax.random.split(jax.random.key(seed), 3)
    return {
        "orbitals": normal_values(streams_of[0], (POINTS, NORB), 1.0, 6.0, ((0, 32),), jnp.float32),
        "points": jnp.clip(1.0 * jax.random.uniform(streams_of[1], (3, POINTS), jnp.float32) ** shard_levels(streams_of[1], (3, POINTS), ((1, 32),), -0.2, 0.2), 0.0, 1.0),
    }


def kernel(near_coords, far_coords):
    squared = jnp.zeros((near_coords.shape[1], far_coords.shape[1]), near_coords.dtype)
    for axis_index in range(3):
        spacing = near_coords[axis_index][:, None] - far_coords[axis_index][None, :]
        squared = squared + spacing * spacing
    return lax.rsqrt(squared + 0.0025)

def reference(orbitals, points):
    point_count = orbitals.shape[0]
    weight = 1.0 / point_count
    highest = lax.Precision.HIGHEST

    def row_block(start_row):
        near_rows = lax.dynamic_slice_in_dim(orbitals, start_row, PTS_DEV, 0)
        near_coords = lax.dynamic_slice_in_dim(points, start_row, PTS_DEV, 1)
        gram_tile = lax.dot_general(near_rows, orbitals, (((1,), (1,)), ((), ())), precision=highest)
        screened = gram_tile * kernel(near_coords, points)
        return -weight * jnp.dot(screened, orbitals, precision=highest)
    starts = (jnp.arange(N_BLK) * PTS_DEV).astype(jnp.int32)
    applied = lax.map(row_block, starts).reshape(point_count, orbitals.shape[1])
    correlation = weight * jnp.dot(orbitals.T, applied, precision=highest)
    factor = jnp.linalg.cholesky(-correlation)
    return lax.linalg.triangular_solve(factor, applied, left_side=False, lower=True, transpose_a=True)
```

```python
import jax
import jax.numpy as jnp
from jax import lax
from jax.sharding import Mesh, PartitionSpec as P

HIGHEST = lax.Precision.HIGHEST
PLANE = ("x", "yh", "yl")


def shift(block, axis, distance):
    size = lax.axis_size(axis)
    return lax.ppermute(block, axis, [(i, (i + distance) % size) for i in range(size)])


def kernel(near_coords, far_coords):
    squared = jnp.zeros((near_coords.shape[1], far_coords.shape[1]), jnp.float32)
    for axis_index in range(3):
        spacing = near_coords[axis_index][:, None] - far_coords[axis_index][None, :]
        squared = squared + spacing * spacing
    return lax.rsqrt(squared + 0.0025)


def gathered(piece, axes):
    copies = jnp.broadcast_to(piece[None], (lax.axis_size(axes),) + piece.shape)
    return lax.all_to_all(copies, axes, 0, 0, tiled=True)


def scattered_sum(parts, axes):
    return jnp.sum(lax.all_to_all(parts, axes, 0, 0, tiled=True), axis=0)


def shards(orbitals, points):
    rows, orbs = orbitals.shape
    core = lax.axis_index("c")
    groups = lax.axis_size(("yh", "x"))
    group = lax.axis_index(("yh", "x"))
    chunk = rows // groups
    weight = 1.0 / (rows * lax.axis_size(("yl", "z", "c")))

    own_rows = lax.dynamic_slice_in_dim(orbitals, group * chunk, chunk, 0)
    own_coords = lax.dynamic_slice_in_dim(points, group * chunk, chunk, 1)
    packed = jnp.concatenate([own_rows, jnp.pad(own_coords, ((0, 5), (0, orbs - chunk)))], axis=0)
    size = packed.shape[0]
    shard = jnp.concatenate([packed, shift(packed, "yl", 1)], axis=0)

    near = jnp.concatenate([orbitals, shift(orbitals, "c", 1)], axis=0)
    near_coords = jnp.concatenate([points, shift(points, "c", 1)], axis=1)

    def unpack(shards_here):
        far, coords = [], []
        for item in shards_here:
            for start in range(0, item.shape[0], size):
                far.append(item[start : start + chunk])
                coords.append(item[start + chunk : start + chunk + 3, :chunk])
        return jnp.concatenate(far, axis=0), jnp.concatenate(coords, axis=1)

    def tile(far, coords):
        gram = lax.dot_general(near, far, (((1,), (1,)), ((), ())), precision=HIGHEST)
        screened = gram * kernel(near_coords, coords)
        return jnp.dot(screened, far, precision=HIGHEST)

    up = down = shard
    ring = lax.axis_size("z")
    partial = tile(*unpack([shard]))
    for step in range(1, ring // 2):
        up, down = shift(up, "z", 1), shift(down, "z", -1)
        partial = partial + tile(*unpack([up, down]))
    last = jnp.concatenate([shift(up[:size], "z", 1), shift(down[size:], "z", -1)], axis=0)
    partial = (partial + tile(*unpack([last]))) * weight

    correlation = weight * lax.dot_general(near, partial, (((0,), (0,)), ((), ())), precision=HIGHEST)
    side = 128
    count = orbs // side
    where = [(i, j) for i in range(count) for j in range(i + 1)]
    lower = jnp.concatenate(
        [correlation[i * side : i * side + side, j * side : j * side + side] for i, j in where], axis=0
    ).reshape(2, -1, side)
    mine = lax.dynamic_index_in_dim(lower, core, 0, keepdims=False)
    other = lax.dynamic_index_in_dim(lower, 1 - core, 0, keepdims=False)
    half = mine + shift(other, "c", 1)
    plane = lax.axis_size(PLANE)
    piece = scattered_sum(half.reshape(plane, -1, side), PLANE)
    piece = jnp.sum(gathered(piece, "z"), axis=0)
    half = gathered(piece, PLANE).reshape(-1, side)
    far_half = shift(half, "c", 1)
    low = jnp.where(core == 0, half, far_half)
    high = jnp.where(core == 0, far_half, half)
    lower = jnp.concatenate([low, high], axis=0).reshape(len(where), side, side)
    lookup = {pair: index for index, pair in enumerate(where)}
    positive = jnp.concatenate(
        [
            jnp.concatenate(
                [lower[lookup[i, j]] if j <= i else lower[lookup[j, i]].T for j in range(count)], axis=1
            )
            for i in range(count)
        ],
        axis=0,
    )

    applied = partial[:rows] + shift(partial[rows:], "c", 1)
    applied = scattered_sum(applied.reshape(groups, chunk, orbs), ("yh", "x"))
    applied = -gathered(applied, ("yh", "x")).reshape(rows, orbs)

    factor = jnp.linalg.cholesky(positive)
    return lax.linalg.triangular_solve(factor, applied, left_side=False, lower=True, transpose_a=True)


def solution(mesh):
    fine = Mesh(mesh.devices.reshape(2, 8, 2, 2, 4), ("yl", "z", "c", "yh", "x"))
    blk = ("yl", "z", "c")
    return jax.shard_map(
        shards,
        mesh=fine,
        in_specs=(P(blk, None), P(None, blk)),
        out_specs=P(blk, None),
        check_vma=False,
    )
```

```python
import jax
import jax.numpy as jnp
from jax import lax
from jax.experimental import pallas as pl
from jax.experimental.pallas import tpu as pltpu
from jax.sharding import Mesh, PartitionSpec as P

HIGHEST = lax.Precision.HIGHEST
SIDE = 128

def lanes(value, index):
    return jnp.broadcast_to(value[:, index : index + 1], (8, SIDE))

def base(a_ref, y_ref, z_ref):
    for strip in range(SIDE // 8):
        start = 8 * strip
        row_a = [jnp.broadcast_to(a_ref[start + i : start + i + 1, :], (8, SIDE)) for i in range(8)]
        row_y = [jnp.broadcast_to(y_ref[start + i : start + i + 1, :], (8, SIDE)) for i in range(8)]
        p = [[None] * 8 for _ in range(8)]
        for i in range(8):
            for k in range(i + 1):
                p[i][k] = p[k][i] = lanes(row_a[i], start + k)
        later = range(strip + 1, SIDE // 8)
        mult = {}
        for t in later:
            block = a_ref[8 * t : 8 * t + 8, :]
            mult[t] = [lanes(block, start + k) for k in range(8)]
        for k in range(8):
            inv = 1.0 / p[k][k]
            root = lax.rsqrt(p[k][k])
            z_ref[start + k : start + k + 1, :] = (row_y[k] * root)[:1]
            for i in range(8):
                if i == k:
                    continue
                for l in range(k + 1, 8):
                    if i > k and l > i:
                        continue
                    p[i][l] = p[i][l] - (p[i][k] * p[k][l]) * inv
                    if i > k:
                        p[l][i] = p[i][l]
            for l in range(k + 1, 8):
                p[k][l] = p[k][l] * inv
            row_a[k] = row_a[k] * inv
            row_y[k] = row_y[k] * inv
            for i in range(8):
                if i != k:
                    row_a[i] = row_a[i] - p[i][k] * row_a[k]
                    row_y[i] = row_y[i] - p[i][k] * row_y[k]
        for t in later:
            for ref, rows in ((a_ref, row_a), (y_ref, row_y)):
                prod = [mult[t][k] * rows[k] for k in range(8)]
                while len(prod) > 1:
                    prod = [prod[i] + prod[i + 1] for i in range(0, len(prod), 2)]
                ref[8 * t : 8 * t + 8, :] = ref[8 * t : 8 * t + 8, :] - prod[0]

def dot(a, b, dims):
    return lax.dot_general(a, b, (dims, ((), ())), precision=HIGHEST, preferred_element_type=jnp.float32)

def chol_kernel(m_ref, z_ref, work, base_a, base_y, base_z):
    n = m_ref.shape[0]
    count = n // SIDE
    work[...] = m_ref[...]
    r = lax.broadcasted_iota(jnp.int32, (n, n), 0)
    c = lax.broadcasted_iota(jnp.int32, (n, n), 1)
    z_ref[...] = jnp.where(r == c, 1.0, 0.0)
    rs = lax.broadcasted_iota(jnp.int32, (SIDE, SIDE), 0)
    cs = lax.broadcasted_iota(jnp.int32, (SIDE, SIDE), 1)
    eye = jnp.where(rs == cs, 1.0, 0.0)
    def step(index, carry):
        off = pl.multiple_of(index * SIDE, SIDE)
        base_a[...] = work[pl.ds(off, SIDE), pl.ds(off, SIDE)]
        base_y[...] = eye
        base(base_a, base_y, base_z)
        zz = base_z[...]
        rows_z = dot(zz, z_ref[pl.ds(off, SIDE), :], ((1,), (0,)))
        z_ref[pl.ds(off, SIDE), :] = rows_z
        upper = dot(zz, work[pl.ds(off, SIDE), :], ((1,), (0,)))
        @pl.when(index < count - 1)
        def _():
            rr = lax.broadcasted_iota(jnp.int32, (SIDE, n), 1)
            keep = jnp.where(rr >= off + SIDE, upper, 0.0)
            work[...] = work[...] - dot(keep, keep, ((0,), (0,)))
            z_ref[...] = z_ref[...] - dot(keep, rows_z, ((0,), (0,)))
        return carry
    lax.fori_loop(0, count, step, 0)

def chol_inverse(m):
    n = m.shape[0]
    return pl.pallas_call(
        chol_kernel,
        out_shape=jax.ShapeDtypeStruct((n, n), jnp.float32),
        in_specs=[pl.BlockSpec(memory_space=pltpu.VMEM)],
        out_specs=pl.BlockSpec(memory_space=pltpu.VMEM),
        scratch_shapes=[pltpu.VMEM((n, n), jnp.float32)] + [pltpu.VMEM((SIDE, SIDE), jnp.float32)] * 3,
        cost_estimate=pl.CostEstimate(flops=2 * 10**10, transcendentals=0, bytes_accessed=2 * 10**6),
    )(m)

PLANE = ("x", "yh", "yl")


def shift(block, axis, distance):
    size = lax.axis_size(axis)
    return lax.ppermute(block, axis, [(i, (i + distance) % size) for i in range(size)])


def point_kernel(near_coords, far_coords):
    squared = jnp.zeros((near_coords.shape[1], far_coords.shape[1]), jnp.float32)
    for axis_index in range(3):
        spacing = near_coords[axis_index][:, None] - far_coords[axis_index][None, :]
        squared = squared + spacing * spacing
    return lax.rsqrt(squared + 0.0025)


def gathered(piece, axes):
    copies = jnp.broadcast_to(piece[None], (lax.axis_size(axes),) + piece.shape)
    return lax.all_to_all(copies, axes, 0, 0, tiled=True)


def scattered_sum(parts, axes):
    return jnp.sum(lax.all_to_all(parts, axes, 0, 0, tiled=True), axis=0)


def shards(orbitals, points):
    rows, orbs = orbitals.shape
    core = lax.axis_index("c")
    groups = lax.axis_size(("yh", "x"))
    group = lax.axis_index(("yh", "x"))
    chunk = rows // groups
    weight = 1.0 / (rows * lax.axis_size(("yl", "z", "c")))

    own_rows = lax.dynamic_slice_in_dim(orbitals, group * chunk, chunk, 0)
    own_coords = lax.dynamic_slice_in_dim(points, group * chunk, chunk, 1)
    packed = jnp.concatenate([own_rows, jnp.pad(own_coords, ((0, 5), (0, orbs - chunk)))], axis=0)
    size = packed.shape[0]
    shard = jnp.concatenate([packed, shift(packed, "yl", 1)], axis=0)

    near = jnp.concatenate([orbitals, shift(orbitals, "c", 1)], axis=0)
    near_coords = jnp.concatenate([points, shift(points, "c", 1)], axis=1)

    def unpack(shards_here):
        far, coords = [], []
        for item in shards_here:
            for start in range(0, item.shape[0], size):
                far.append(item[start : start + chunk])
                coords.append(item[start + chunk : start + chunk + 3, :chunk])
        return jnp.concatenate(far, axis=0), jnp.concatenate(coords, axis=1)

    def tile(far, coords):
        gram = lax.dot_general(near, far, (((1,), (1,)), ((), ())), precision=HIGHEST)
        screened = gram * point_kernel(near_coords, coords)
        return jnp.dot(screened, far, precision=HIGHEST)

    up = down = shard
    ring = lax.axis_size("z")
    partial = tile(*unpack([shard]))
    up, down, partial = lax.optimization_barrier((shift(up, "z", 1), shift(down, "z", -1), partial))
    for step in range(2, ring // 2):
        ahead = shift(up, "z", 1), shift(down, "z", -1)
        partial = partial + tile(*unpack([up, down]))
        up, down, partial = lax.optimization_barrier((*ahead, partial))
    ahead = shift(up[:size], "z", 1), shift(down[size:], "z", -1)
    partial = partial + tile(*unpack([up, down]))
    up, down, partial = lax.optimization_barrier((*ahead, partial))
    partial = (partial + tile(*unpack([up, down]))) * weight

    correlation = weight * lax.dot_general(near, partial, (((0,), (0,)), ((), ())), precision=HIGHEST)
    side = 128
    count = orbs // side
    where = [(i, j) for i in range(count) for j in range(i + 1)]
    lower = jnp.concatenate(
        [correlation[i * side : i * side + side, j * side : j * side + side] for i, j in where], axis=0
    ).reshape(2, -1, side)
    mine = lax.dynamic_index_in_dim(lower, core, 0, keepdims=False)
    other = lax.dynamic_index_in_dim(lower, 1 - core, 0, keepdims=False)
    half = mine + shift(other, "c", 1)
    applied = partial[:rows] + shift(partial[rows:], "c", 1)
    plane = lax.axis_size(PLANE)
    piece = scattered_sum(half.reshape(plane, -1, side), PLANE)
    piece, applied = lax.optimization_barrier((piece, applied))
    applied = scattered_sum(applied.reshape(groups, chunk, orbs), ("yh", "x"))
    piece = jnp.sum(gathered(piece, "z"), axis=0)
    half = gathered(piece, PLANE).reshape(-1, side)
    far_half = shift(half, "c", 1)
    low = jnp.where(core == 0, half, far_half)
    high = jnp.where(core == 0, far_half, half)
    lower = jnp.concatenate([low, high], axis=0).reshape(len(where), side, side)
    lookup = {pair: index for index, pair in enumerate(where)}
    positive = jnp.concatenate(
        [
            jnp.concatenate(
                [lower[lookup[i, j]] if j <= i else lower[lookup[j, i]].T for j in range(count)], axis=1
            )
            for i in range(count)
        ],
        axis=0,
    )

    positive, applied = lax.optimization_barrier((positive, applied))
    applied = gathered(applied, ("yh", "x")).reshape(rows, orbs)
    inverse = chol_inverse(positive)
    return -lax.dot_general(applied, inverse, (((1,), (1,)), ((), ())), precision=HIGHEST)


def solution(mesh):
    fine = Mesh(mesh.devices.reshape(2, 8, 2, 2, 4), ("yl", "z", "c", "yh", "x"))
    blk = ("yl", "z", "c")
    return jax.shard_map(
        shards,
        mesh=fine,
        in_specs=(P(blk, None), P(None, blk)),
        out_specs=P(blk, None),
        check_vma=False,
    )
```

```python
import jax
import jax.numpy as jnp
from jax import lax
from jax.experimental import pallas as pl
from jax.experimental.pallas import tpu as pltpu
from jax.sharding import Mesh, PartitionSpec as P

HIGHEST = lax.Precision.HIGHEST
HIGH = lax.Precision.HIGH
PLANE = ("x", "yh", "yl")
SIDE = 128

def lanes(value, index):
    return jnp.broadcast_to(value[:, index : index + 1], (8, SIDE))

def base(a_ref, y_ref, z_ref):
    for strip in range(SIDE // 8):
        start = 8 * strip
        row_a = [jnp.broadcast_to(a_ref[start + i : start + i + 1, :], (8, SIDE)) for i in range(8)]
        row_y = [jnp.broadcast_to(y_ref[start + i : start + i + 1, :], (8, SIDE)) for i in range(8)]
        p = [[None] * 8 for _ in range(8)]
        for i in range(8):
            for k in range(i + 1):
                p[i][k] = p[k][i] = lanes(row_a[i], start + k)
        later = range(strip + 1, SIDE // 8)
        mult = {}
        for t in later:
            block = a_ref[8 * t : 8 * t + 8, :]
            mult[t] = [lanes(block, start + k) for k in range(8)]
        for k in range(8):
            inv = 1.0 / p[k][k]
            root = lax.rsqrt(p[k][k])
            z_ref[start + k : start + k + 1, :] = (row_y[k] * root)[:1]
            for i in range(8):
                if i == k:
                    continue
                for l in range(k + 1, 8):
                    if i > k and l > i:
                        continue
                    p[i][l] = p[i][l] - (p[i][k] * p[k][l]) * inv
                    if i > k:
                        p[l][i] = p[i][l]
            for l in range(k + 1, 8):
                p[k][l] = p[k][l] * inv
            row_a[k] = row_a[k] * inv
            row_y[k] = row_y[k] * inv
            for i in range(8):
                if i != k:
                    row_a[i] = row_a[i] - p[i][k] * row_a[k]
                    row_y[i] = row_y[i] - p[i][k] * row_y[k]
        for t in later:
            for ref, rows in ((a_ref, row_a), (y_ref, row_y)):
                prod = [mult[t][k] * rows[k] for k in range(8)]
                while len(prod) > 1:
                    prod = [prod[i] + prod[i + 1] for i in range(0, len(prod), 2)]
                ref[8 * t : 8 * t + 8, :] = ref[8 * t : 8 * t + 8, :] - prod[0]


def dot(a, b, dims, precision=HIGHEST):
    return lax.dot_general(a, b, (dims, ((), ())), precision=precision, preferred_element_type=jnp.float32)


def chol_kernel(m_ref, z_ref, work, rows, base_a, base_y, base_z):
    n = m_ref.shape[0]
    count = n // SIDE
    work[:, :n] = m_ref[...]
    row = lax.broadcasted_iota(jnp.int32, (n, n), 0)
    column = lax.broadcasted_iota(jnp.int32, (n, n), 1)
    work[:, n:] = jnp.where(row == column, 1.0, 0.0)
    row = lax.broadcasted_iota(jnp.int32, (SIDE, SIDE), 0)
    column = lax.broadcasted_iota(jnp.int32, (SIDE, SIDE), 1)
    eye = jnp.where(row == column, 1.0, 0.0)

    def step(index, carry):
        here = pl.ds(pl.multiple_of(index * SIDE, SIDE), SIDE)
        base_a[...] = work[here, here]
        base_y[...] = eye
        base(base_a, base_y, base_z)
        rows[...] = dot(base_z[...], work[here, :], ((1,), (0,)))
        z_ref[here, :] = rows[:, n:]

        def update(later, inner):
            there = pl.ds(pl.multiple_of(later * SIDE, SIDE), SIDE)
            work[there, :] = work[there, :] - dot(rows[:, there], rows[...], ((0,), (0,)))
            return inner

        lax.fori_loop(index + 1, count, update, 0)
        return carry

    lax.fori_loop(0, count, step, 0)


def chol_inverse(m):
    n = m.shape[0]
    return pl.pallas_call(
        chol_kernel,
        out_shape=jax.ShapeDtypeStruct((n, n), jnp.float32),
        in_specs=[pl.BlockSpec(memory_space=pltpu.VMEM)],
        out_specs=pl.BlockSpec(memory_space=pltpu.VMEM),
        scratch_shapes=[pltpu.VMEM((n, 2 * n), jnp.float32), pltpu.VMEM((SIDE, 2 * n), jnp.float32)]
        + [pltpu.VMEM((SIDE, SIDE), jnp.float32)] * 3,
        cost_estimate=pl.CostEstimate(flops=2 * 10**10, transcendentals=0, bytes_accessed=2 * 10**6),
    )(m)


def shift(block, axis, distance):
    size = lax.axis_size(axis)
    return lax.ppermute(block, axis, [(i, (i + distance) % size) for i in range(size)])


def shift_y(block, distance):
    size = lax.axis_size(("yl", "yh"))
    place = [(y % 2) * (size // 2) + y // 2 for y in range(size)]
    return lax.ppermute(block, ("yl", "yh"), [(place[y], place[(y + distance) % size]) for y in range(size)])


def point_kernel(near_coords, far_coords):
    squared = jnp.zeros((near_coords.shape[1], far_coords.shape[1]), jnp.float32)
    for axis_index in range(3):
        spacing = near_coords[axis_index][:, None] - far_coords[axis_index][None, :]
        squared = squared + spacing * spacing
    return lax.rsqrt(squared + 0.0025)


def gathered(piece, axes):
    copies = jnp.broadcast_to(piece[None], (lax.axis_size(axes),) + piece.shape)
    return lax.all_to_all(copies, axes, 0, 0, tiled=True)


def scattered_sum(parts, axes):
    return jnp.sum(lax.all_to_all(parts, axes, 0, 0, tiled=True), axis=0)


def packed(rows, coords):
    return jnp.concatenate([rows, jnp.pad(coords, ((0, 5), (0, rows.shape[1] - coords.shape[1])))], axis=0)


def unpacked(pieces):
    size = pieces[0].shape[0] - 8
    rows = jnp.concatenate([piece[:size] for piece in pieces], axis=0)
    return rows, jnp.concatenate([piece[size : size + 3, :size] for piece in pieces], axis=1)


def shards(orbitals, points):
    rows, orbs = orbitals.shape
    core = lax.axis_index("c")
    groups = lax.axis_size(("yh", "x"))
    group = lax.axis_index(("yh", "x"))
    chunk = rows // groups
    weight = 1.0 / (rows * lax.axis_size(("yl", "z", "c")))
    barrier = lax.optimization_barrier

    own = packed(
        lax.dynamic_slice_in_dim(orbitals, group * chunk, chunk, 0),
        lax.dynamic_slice_in_dim(points, group * chunk, chunk, 1),
    )
    middle = rows // 2
    from_below = shift_y(packed(orbitals[:middle], points[:, :middle]), 1)
    from_above = shift_y(packed(orbitals[middle:], points[:, middle:]), -1)
    up, down, own_pair = shift(own, "z", 1), shift(own, "z", -1), jnp.stack([own, shift(own, "c", 1)])
    up, down, own_pair, from_below, from_above = barrier((up, down, own_pair, from_below, from_above))
    partner, partner_coords = unpacked([from_below, from_above])
    near = jnp.concatenate([orbitals, partner], axis=0)
    near_coords = jnp.concatenate([points, partner_coords], axis=1)

    def tile(pieces):
        far, coords = unpacked(pieces)
        gram = dot(near, far, ((1,), (1,)), HIGH)
        return dot(gram * point_kernel(near_coords, coords), far, ((1,), (0,)), HIGH)

    def both_cores(block):
        return [block, shift(block, "c", 1)]

    ring = lax.axis_size("z")
    partial = None
    held = [own_pair[0], own_pair[1]]
    for step in range(2, ring // 2 + 1):
        if step < ring // 2:
            ahead = shift(up, "z", 1), shift(down, "z", -1)
        else:
            half = own.shape[0] // 16 * 8 + 8
            ahead = shift(up[:half], "z", 1), shift(down[half:], "z", -1)
        pieces = both_cores(up) + both_cores(down)
        if step == 2:
            pieces = held + pieces
        product = tile(pieces)
        partial = product if partial is None else partial + product
        up, down, partial = barrier((*ahead, partial))
    partial = (partial + tile(both_cores(jnp.concatenate([up, down], axis=0)))) * weight

    to_above = shift_y(partial[rows : rows + middle], 1)
    to_below = shift_y(partial[rows + middle :], -1)

    correlation = weight * dot(near, partial, ((0,), (0,)), HIGH)
    side = 128
    count = orbs // side
    where = [(i, j) for i in range(count) for j in range(i + 1)]
    lower = jnp.concatenate(
        [correlation[i * side : i * side + side, j * side : j * side + side] for i, j in where], axis=0
    ).reshape(2, -1, side)
    mine = lax.dynamic_index_in_dim(lower, core, 0, keepdims=False)
    other = lax.dynamic_index_in_dim(lower, 1 - core, 0, keepdims=False)
    half = mine + shift(other, "c", 1)
    plane = lax.axis_size(PLANE)
    piece = scattered_sum(half.reshape(plane, -1, side), PLANE)
    piece, to_above, to_below = barrier((piece, to_above, to_below))

    applied = partial[:rows] + jnp.concatenate([to_above, to_below], axis=0)
    lines = lax.axis_size("x")
    line, yh = lax.axis_index("x"), lax.axis_index("yh")
    by_line = applied.reshape(groups // lines, lines, chunk, orbs)
    parts = [lax.dynamic_index_in_dim(by_line, line, 1, keepdims=False)]
    for distance in range(1, lines):
        part = lax.dynamic_index_in_dim(by_line, (line + distance) % lines, 1, keepdims=False)
        parts.append(shift(part, "x", distance))
    piece = jnp.sum(gathered(piece, "z"), axis=0)
    piece, *parts = barrier((piece, *parts))
    pair = sum(parts[1:], parts[0])
    kept = lax.dynamic_index_in_dim(pair, yh, 0, keepdims=False)
    sent = shift(lax.dynamic_index_in_dim(pair, 1 - yh, 0, keepdims=False), "yh", 1)

    half = gathered(piece, PLANE).reshape(-1, side)
    half, kept, sent = barrier((half, kept, sent))
    applied = kept + sent
    far_half = shift(half, "c", 1)
    low = jnp.where(core == 0, half, far_half)
    high = jnp.where(core == 0, far_half, half)
    lower = jnp.concatenate([low, high], axis=0).reshape(len(where), side, side)
    lookup = {pair: index for index, pair in enumerate(where)}
    positive = jnp.concatenate(
        [
            jnp.concatenate(
                [lower[lookup[i, j]] if j <= i else lower[lookup[j, i]].T for j in range(count)], axis=1
            )
            for i in range(count)
        ],
        axis=0,
    )
    positive, applied = barrier((positive, applied))
    applied = gathered(applied, ("yh", "x")).reshape(rows, orbs)
    inverse = chol_inverse(positive)
    return -dot(applied, inverse, ((1,), (1,)), HIGH)


def solution(mesh):
    fine = Mesh(mesh.devices.reshape(2, 8, 2, 2, 4), ("yl", "z", "c", "yh", "x"))
    blk = ("yl", "z", "c")
    return jax.shard_map(
        shards,
        mesh=fine,
        in_specs=(P(blk, None), P(None, blk)),
        out_specs=P(blk, None),
        check_vma=False,
    )
```

```python
import functools

import jax
import jax.numpy as jnp
from jax import lax
from jax.experimental import pallas as pl
from jax.experimental.pallas import tpu as pltpu
from jax.sharding import Mesh, PartitionSpec as P

HIGHEST = lax.Precision.HIGHEST
PLANE = ("x", "yh", "yl")

SIDE = 128


def lanes(value, index):
    return jnp.broadcast_to(value[:, index : index + 1], (8, SIDE))


def base(a_ref, z_ref, spread):
    strips = SIDE // 8
    lane = lax.broadcasted_iota(jnp.int32, (8, SIDE), 1)

    def opened(strip, block):
        start = 8 * strip
        inside = (lane >= start) & (lane < start + 8)
        for k in range(8):
            spread[8 * k : 8 * k + 8, :] = lanes(block, start + k)
        p = [[None] * 8 for _ in range(8)]
        for i in range(8):
            for k in range(i + 1):
                p[i][k] = p[k][i] = jnp.broadcast_to(spread[8 * k + i : 8 * k + i + 1, :], (8, SIDE))
        row = [jnp.broadcast_to(a_ref[start + i : start + i + 1, :], (8, SIDE)) for i in range(8)]
        row = [jnp.where(inside, jnp.where(lane == start + i, 1.0, 0.0), row[i]) for i in range(8)]
        return start, inside, row, p

    def update(strip, later, inside, row):
        there = slice(8 * later, 8 * later + 8)
        block = a_ref[there, :]
        product = [lanes(block, 8 * strip + k) * row[k] for k in range(8)]
        while len(product) > 1:
            product = [product[i] + product[i + 1] for i in range(0, len(product), 2)]
        block = jnp.where(inside, 0.0, block) - product[0]
        a_ref[there, :] = block
        return block

    state = opened(0, a_ref[:8, :])
    for strip in range(strips):
        start, inside, row, p = state
        for k in range(8):
            inv = 1.0 / p[k][k]
            z_ref[start + k : start + k + 1, :] = (row[k] * lax.rsqrt(p[k][k]))[:1]
            scaled = [None if i == k else p[i][k] * inv for i in range(8)]
            for i in list(range(k + 1, 8)) + list(range(k)):
                for l in range(k + 1, 8):
                    if i > k and l > i:
                        continue
                    if i == l == k + 1:
                        p[i][l] = p[i][l] - (p[i][k] * p[k][l]) * inv
                    else:
                        p[i][l] = p[i][l] - scaled[i] * p[k][l]
                    if i > k:
                        p[l][i] = p[i][l]
            for l in range(k + 1, 8):
                p[k][l] = scaled[l] if l > k else p[k][l]
            for i in range(8):
                if i != k:
                    row[i] = row[i] - scaled[i] * row[k]
            row[k] = row[k] * inv
        if strip + 1 < strips:
            state = opened(strip + 1, update(strip, strip + 1, inside, row))
        for later in range(strip + 2, strips):
            update(strip, later, inside, row)


def dot(a, b, dims, precision=HIGHEST):
    return lax.dot_general(a, b, (dims, ((), ())), precision=precision, preferred_element_type=jnp.float32)


def split(value):
    upper = value.astype(jnp.bfloat16)
    return upper, (value - upper.astype(jnp.float32)).astype(jnp.bfloat16)


def dot_split(a, b, dims):
    return dot(a[0], b[0], dims, None) + (dot(a[0], b[1], dims, None) + dot(a[1], b[0], dims, None))


def chol_kernel(core_ref, mine_ref, other_ref, z_ref, rows, base_a, base_z, spread):
    n = z_ref.shape[0]
    count = n // SIDE
    where = [(i, j) for i in range(count) for j in range(i, count)]
    each = len(where) // 2
    for number, (i, j) in enumerate(where):
        here = slice(number % each * SIDE, number % each * SIDE + SIDE)
        block = jnp.where(core_ref[0] == number // each, mine_ref[here, :], other_ref[here, :])
        z_ref[i * SIDE : i * SIDE + SIDE, j * SIDE : j * SIDE + SIDE] = block
        if i < j:
            z_ref[j * SIDE : j * SIDE + SIDE, i * SIDE : i * SIDE + SIDE] = jnp.zeros((SIDE, SIDE), jnp.float32)
    row = lax.broadcasted_iota(jnp.int32, (SIDE, SIDE), 0)
    column = lax.broadcasted_iota(jnp.int32, (SIDE, SIDE), 1)
    eye = jnp.where(row == column, 1.0, 0.0)

    def step(index, carry):
        here = pl.ds(pl.multiple_of(index * SIDE, SIDE), SIDE)
        base_a[...] = z_ref[here, here]
        base(base_a, base_z, spread)
        z_ref[here, here] = eye
        lower = jnp.where(row >= column, base_z[...], 0.0)
        rows[...] = dot(lower, z_ref[here, :], ((1,), (0,)))
        z_ref[here, :] = rows[...]

        def update(later, inner):
            there = pl.ds(pl.multiple_of(later * SIDE, SIDE), SIDE)
            z_ref[there, here] = jnp.zeros((SIDE, SIDE), jnp.float32)
            z_ref[there, :] = z_ref[there, :] - dot(rows[:, there], rows[...], ((0,), (0,)))
            return inner

        lax.fori_loop(index + 1, count, update, 0)
        return carry

    lax.fori_loop(0, count, step, 0)
    for i in range(count):
        for j in range(i + 1, count):
            z_ref[i * SIDE : i * SIDE + SIDE, j * SIDE : j * SIDE + SIDE] = jnp.zeros((SIDE, SIDE), jnp.float32)


def call(body, out_shape, scratch, aliases, flops, scalars, *operands):
    vmem = pl.BlockSpec(memory_space=pltpu.VMEM)
    smem = pl.BlockSpec(memory_space=pltpu.SMEM)
    return pl.pallas_call(
        body,
        out_shape=out_shape,
        in_specs=[smem] * scalars + [vmem] * (len(operands) - scalars),
        out_specs=jax.tree.map(lambda _: vmem, out_shape),
        scratch_shapes=scratch,
        input_output_aliases=aliases,
        cost_estimate=pl.CostEstimate(flops=flops, transcendentals=0, bytes_accessed=2 * 10**6),
    )(*operands)


def chol_inverse(core, mine, other, n):
    scratch = [pltpu.VMEM(s, jnp.float32) for s in ((SIDE, n), (SIDE, SIDE), (SIDE, SIDE), (64, SIDE))]
    return call(chol_kernel, jax.ShapeDtypeStruct((n, n), jnp.float32), scratch, {}, 2 * 10**10, 1, core, mine, other)


def near_kernel(own_ref, points_ref, below_ref, above_ref, hi_ref, lo_ref, turned_hi_ref, turned_lo_ref, spread_ref):
    rows = own_ref.shape[0]
    middle = rows // 2
    parts = [
        (0, rows, own_ref, points_ref, 0),
        (rows, middle, below_ref, below_ref, middle),
        (rows + middle, middle, above_ref, above_ref, middle),
    ]
    for start, size, ref, coords, first in parts:
        for at in range(0, size, middle):
            value = ref[at : at + middle, :]
            there = slice(start + at, start + at + middle)
            hi_ref[there, :], lo_ref[there, :] = split(value)
            turned_hi_ref[:, there], turned_lo_ref[:, there] = split(value.T)
            for k in range(3):
                line = coords[first + k : first + k + 1, at : at + middle]
                spread_ref[k, there, :] = jnp.broadcast_to(line, (SIDE, middle)).T


def add_tile(near, acc, out, pieces, far_hi, far_lo, slab):
    hi_ref, lo_ref, spread_ref = near
    chunk = pieces[0].shape[0] - 8
    lane = lax.broadcasted_iota(jnp.int32, (8, SIDE), 1)
    for number, piece in enumerate(pieces):
        there = slice(number * chunk, number * chunk + chunk)
        far_hi[there, :], far_lo[there, :] = split(piece[:chunk, :])
    for number in range(0, len(pieces), 2):
        left, right = (pieces[number + i][chunk : chunk + 8, :SIDE] for i in range(2))
        at = number * chunk
        slab[:, at : at + SIDE] = jnp.where(lane < chunk, left, pltpu.roll(right, chunk, 1))
    step = 256
    width = len(pieces) * chunk

    def block(index, carry):
        here = pl.ds(pl.multiple_of(index * step, step), step)
        gram = dot_split((hi_ref[here, :], lo_ref[here, :]), (far_hi[...], far_lo[...]), ((1,), (1,)))
        squares = []
        for at in range(0, width, SIDE):
            square = 0.0025
            for k in range(3):
                spacing = spread_ref[k, here, :] - slab[k : k + 1, at : at + SIDE]
                square = square + spacing * spacing
            squares.append(square)
        screened = gram * lax.rsqrt(jnp.concatenate(squares, axis=1))
        product = dot_split(split(screened), (far_hi[...], far_lo[...]), ((1,), (0,)))
        out[here, :] = product if acc is None else acc[here, :] + product
        return carry

    lax.fori_loop(0, hi_ref.shape[0] // step, block, 0)


def first_kernel(pieces, *refs):
    near, found, out, scratch = refs[:3], refs[3 : 3 + pieces], refs[3 + pieces], refs[4 + pieces :]
    add_tile(near, None, out, found, *scratch)


def tile_kernel(pieces, *refs):
    near, acc, found, out, scratch = refs[:3], refs[3], refs[4 : 4 + pieces], refs[4 + pieces], refs[5 + pieces :]
    add_tile(near, acc, out, found, *scratch)


def last_kernel(pieces, weight, core_ref, *refs):
    near, turned, acc, found = refs[:3], refs[3:5], refs[5], refs[6 : 6 + pieces]
    own_ref, below_ref, above_ref, mine_ref, other_ref, total, total_hi, total_lo = refs[6 + pieces : 14 + pieces]
    add_tile(near, acc, total, found, *refs[14 + pieces :])
    rows = own_ref.shape[0]
    middle = rows // 2
    own_ref[...] = total[:rows, :] * weight
    below_ref[...] = total[rows : rows + middle, :] * weight
    above_ref[...] = total[rows + middle :, :] * weight
    total_hi[...], total_lo[...] = split(total[...])
    count = total.shape[1] // SIDE
    number = 0
    each = count * (count + 1) // 4
    for i in range(count):
        left = tuple(ref[i * SIDE : i * SIDE + SIDE, :] for ref in turned)
        wide = dot_split(left, (total_hi[:, i * SIDE :], total_lo[:, i * SIDE :]), ((1,), (0,))) * (weight * weight)
        for j in range(i, count):
            block = wide[:, (j - i) * SIDE : (j - i) * SIDE + SIDE]
            there = slice(number % each * SIDE, number % each * SIDE + SIDE)

            @pl.when(core_ref[0] == number // each)
            def _():
                mine_ref[there, :] = block

            @pl.when(core_ref[0] != number // each)
            def _():
                other_ref[there, :] = block

            number += 1


def shift(block, axis, distance):
    size = lax.axis_size(axis)
    return lax.ppermute(block, axis, [(i, (i + distance) % size) for i in range(size)])


def shift_y(block, distance):
    size = lax.axis_size(("yl", "yh"))
    place = [(y % 2) * (size // 2) + y // 2 for y in range(size)]
    return lax.ppermute(block, ("yl", "yh"), [(place[y], place[(y + distance) % size]) for y in range(size)])


def gathered(piece, axes):
    copies = jnp.broadcast_to(piece[None], (lax.axis_size(axes),) + piece.shape)
    return lax.all_to_all(copies, axes, 0, 0, tiled=True)


def scattered_sum(parts, axes):
    return jnp.sum(lax.all_to_all(parts, axes, 0, 0, tiled=True), axis=0)


def packed(rows, coords):
    return jnp.concatenate([rows, jnp.pad(coords, ((0, 5), (0, rows.shape[1] - coords.shape[1])))], axis=0)


def shards(orbitals, points):
    rows, orbs = orbitals.shape
    core = lax.axis_index("c")
    core_ref = core.astype(jnp.int32)[None]
    groups = lax.axis_size(("yh", "x"))
    group = lax.axis_index(("yh", "x"))
    chunk = rows // groups
    weight = 1.0 / (rows * lax.axis_size(("yl", "z", "c")))
    barrier = lax.optimization_barrier

    own = packed(
        lax.dynamic_slice_in_dim(orbitals, group * chunk, chunk, 0),
        lax.dynamic_slice_in_dim(points, group * chunk, chunk, 1),
    )
    middle = rows // 2
    from_below = shift_y(packed(orbitals[:middle], points[:, :middle]), 1)
    from_above = shift_y(packed(orbitals[middle:], points[:, middle:]), -1)
    far = {0: own}
    ring = lax.axis_size("z")
    order = [0]
    for distance in range(1, ring // 2):
        order += [distance, -distance]
    order.append(ring // 2)
    for distance in order[1:]:
        far[distance] = shift(own, "z", distance)

    tall = 2 * rows
    half_type = jax.ShapeDtypeStruct((tall, orbs), jnp.bfloat16)
    turned_type = jax.ShapeDtypeStruct((orbs, tall), jnp.bfloat16)
    spread_type = jax.ShapeDtypeStruct((3, tall, SIDE), jnp.float32)
    near_hi, near_lo, turned_hi, turned_lo, spread = call(
        near_kernel, (half_type, half_type, turned_type, turned_type, spread_type), [], {}, 10**9, 0,
        orbitals, points, from_below, from_above,
    )
    near = (near_hi, near_lo, spread)

    def scratch(pieces):
        wide = pieces * chunk
        return [pltpu.VMEM((wide, orbs), jnp.bfloat16)] * 2 + [pltpu.VMEM((8, wide), jnp.float32)]

    total_type = jax.ShapeDtypeStruct((tall, orbs), jnp.float32)
    stages = [order[:3], order[3:5], order[5:7], order[7:]]
    total = None
    for number, stage in enumerate(stages[:-1]):
        pieces = []
        for distance in stage:
            pieces += [far[distance], shift(far[distance], "c", 1)]
        count = len(pieces)
        if number == 0:
            body = functools.partial(first_kernel, count)
            total = call(body, total_type, scratch(count), {}, 4 * 10**9, 0, *near, *pieces)
        else:
            body = functools.partial(tile_kernel, count)
            total = call(body, total_type, scratch(count), {3: 0}, 3 * 10**9, 0, *near, total, *pieces)
    pieces = []
    for distance in stages[-1]:
        pieces += [far[distance], shift(far[distance], "c", 1)]
    count = len(pieces)
    tri = (orbs // SIDE) * (orbs // SIDE + 1) // 4 * SIDE
    middle_type = jax.ShapeDtypeStruct((middle, orbs), jnp.float32)
    tri_type = jax.ShapeDtypeStruct((tri, SIDE), jnp.float32)
    own_part, to_above, to_below, mine, other = call(
        functools.partial(last_kernel, count, weight),
        (jax.ShapeDtypeStruct((rows, orbs), jnp.float32), middle_type, middle_type, tri_type, tri_type),
        [pltpu.VMEM((tall, orbs), jnp.float32)] + [pltpu.VMEM((tall, orbs), jnp.bfloat16)] * 2 + scratch(count),
        {}, 3 * 10**9, 1, core_ref, *near, turned_hi, turned_lo, total, *pieces,
    )

    half = mine + shift(other, "c", 1)
    to_above = shift_y(to_above, 1)
    to_below = shift_y(to_below, -1)
    plane = lax.axis_size(PLANE)
    piece = scattered_sum(half.reshape(plane, -1, SIDE), PLANE)
    piece, to_above, to_below = barrier((piece, to_above, to_below))

    applied = own_part + jnp.concatenate([to_above, to_below], axis=0)
    lines = lax.axis_size("x")
    line, yh = lax.axis_index("x"), lax.axis_index("yh")
    by_line = applied.reshape(groups // lines, lines, chunk, orbs)
    parts = [lax.dynamic_index_in_dim(by_line, line, 1, keepdims=False)]
    for distance in range(1, lines):
        part = lax.dynamic_index_in_dim(by_line, (line + distance) % lines, 1, keepdims=False)
        parts.append(shift(part, "x", distance))
    piece = jnp.sum(gathered(piece, "z"), axis=0)
    pair = sum(parts[1:], parts[0])
    kept = lax.dynamic_index_in_dim(pair, yh, 0, keepdims=False)
    sent = shift(lax.dynamic_index_in_dim(pair, 1 - yh, 0, keepdims=False), "yh", 1)

    half = gathered(piece, PLANE).reshape(-1, SIDE)
    half, kept, sent = barrier((half, kept, sent))
    applied = kept + sent
    far_half, applied = barrier((shift(half, "c", 1), applied))
    applied = gathered(applied, ("yh", "x")).reshape(rows, orbs)
    inverse = chol_inverse(core_ref, half, far_half, orbs)
    return -dot(applied, inverse, ((1,), (1,)))


def solution(mesh):
    fine = Mesh(mesh.devices.reshape(2, 8, 2, 2, 4), ("yl", "z", "c", "yh", "x"))
    blk = ("yl", "z", "c")
    return jax.shard_map(
        shards,
        mesh=fine,
        in_specs=(P(blk, None), P(None, blk)),
        out_specs=P(blk, None),
        check_vma=False,
    )
```

```python
import functools

import jax
import jax.numpy as jnp
from jax import lax
from jax.experimental import pallas as pl
from jax.experimental.pallas import tpu as pltpu
from jax.sharding import Mesh, PartitionSpec as P


HIGHEST = lax.Precision.HIGHEST
PLANE = ("x", "yh", "yl")

SIDE = 128


def lanes(value, index):
    return jnp.broadcast_to(value[:, index : index + 1], (8, SIDE))


def base(a_ref, z_ref, spread):
    strips = SIDE // 8
    lane = lax.broadcasted_iota(jnp.int32, (8, SIDE), 1)

    def opened(strip, block):
        start = 8 * strip
        inside = (lane >= start) & (lane < start + 8)
        for k in range(8):
            spread[8 * k : 8 * k + 8, :] = lanes(block, start + k)
        p = [[None] * 8 for _ in range(8)]
        for i in range(8):
            for k in range(i + 1):
                p[i][k] = p[k][i] = jnp.broadcast_to(spread[8 * k + i : 8 * k + i + 1, :], (8, SIDE))
        row = [jnp.broadcast_to(a_ref[start + i : start + i + 1, :], (8, SIDE)) for i in range(8)]
        row = [jnp.where(inside, jnp.where(lane == start + i, 1.0, 0.0), row[i]) for i in range(8)]
        return start, inside, row, p

    def update(strip, later, inside, row):
        there = slice(8 * later, 8 * later + 8)
        block = a_ref[there, :]
        product = [lanes(block, 8 * strip + k) * row[k] for k in range(8)]
        while len(product) > 1:
            product = [product[i] + product[i + 1] for i in range(0, len(product), 2)]
        block = jnp.where(inside, 0.0, block) - product[0]
        a_ref[there, :] = block
        return block

    state = opened(0, a_ref[:8, :])
    for strip in range(strips):
        start, inside, row, p = state
        for k in range(8):
            inv = 1.0 / p[k][k]
            z_ref[start + k : start + k + 1, :] = (row[k] * lax.rsqrt(p[k][k]))[:1]
            scaled = [None if i == k else p[i][k] * inv for i in range(8)]
            for i in list(range(k + 1, 8)) + list(range(k)):
                for l in range(k + 1, 8):
                    if i > k and l > i:
                        continue
                    if i == l == k + 1:
                        p[i][l] = p[i][l] - (p[i][k] * p[k][l]) * inv
                    else:
                        p[i][l] = p[i][l] - scaled[i] * p[k][l]
                    if i > k:
                        p[l][i] = p[i][l]
            for l in range(k + 1, 8):
                p[k][l] = scaled[l] if l > k else p[k][l]
            for i in range(8):
                if i != k:
                    row[i] = row[i] - scaled[i] * row[k]
            row[k] = row[k] * inv
        if strip + 1 < strips:
            state = opened(strip + 1, update(strip, strip + 1, inside, row))
        for later in range(strip + 2, strips):
            update(strip, later, inside, row)


def dot(a, b, dims, precision=HIGHEST):
    return lax.dot_general(a, b, (dims, ((), ())), precision=precision, preferred_element_type=jnp.float32)


def split(value):
    upper = value.astype(jnp.bfloat16)
    return upper, (value - upper.astype(jnp.float32)).astype(jnp.bfloat16)


def chol_kernel(core_ref, mine_ref, other_ref, z_ref, rows, base_a, base_z, spread):
    n = z_ref.shape[0]
    count = n // SIDE
    where = [(i, j) for i in range(count) for j in range(i, count)]
    each = len(where) // 2
    for number, (i, j) in enumerate(where):
        here = slice(number % each * SIDE, number % each * SIDE + SIDE)
        block = jnp.where(core_ref[0] == number // each, mine_ref[here, :], other_ref[here, :])
        z_ref[i * SIDE : i * SIDE + SIDE, j * SIDE : j * SIDE + SIDE] = block
        if i < j:
            z_ref[j * SIDE : j * SIDE + SIDE, i * SIDE : i * SIDE + SIDE] = jnp.zeros((SIDE, SIDE), jnp.float32)
    row = lax.broadcasted_iota(jnp.int32, (SIDE, SIDE), 0)
    column = lax.broadcasted_iota(jnp.int32, (SIDE, SIDE), 1)
    eye = jnp.where(row == column, 1.0, 0.0)

    def step(index, carry):
        here = pl.ds(pl.multiple_of(index * SIDE, SIDE), SIDE)
        base_a[...] = z_ref[here, here]
        base(base_a, base_z, spread)
        z_ref[here, here] = eye
        lower = jnp.where(row >= column, base_z[...], 0.0)
        rows[...] = dot(lower, z_ref[here, :], ((1,), (0,)))
        z_ref[here, :] = rows[...]

        def update(later, inner):
            there = pl.ds(pl.multiple_of(later * SIDE, SIDE), SIDE)
            z_ref[there, here] = jnp.zeros((SIDE, SIDE), jnp.float32)
            z_ref[there, :] = z_ref[there, :] - dot(rows[:, there], rows[...], ((0,), (0,)))
            return inner

        lax.fori_loop(index + 1, count, update, 0)
        return carry

    lax.fori_loop(0, count, step, 0)
    for i in range(count):
        for j in range(i + 1, count):
            z_ref[i * SIDE : i * SIDE + SIDE, j * SIDE : j * SIDE + SIDE] = jnp.zeros((SIDE, SIDE), jnp.float32)


def call(body, out_shape, scratch, aliases, flops, scalars, *operands):
    vmem = pl.BlockSpec(memory_space=pltpu.VMEM)
    smem = pl.BlockSpec(memory_space=pltpu.SMEM)
    return pl.pallas_call(
        body,
        out_shape=out_shape,
        in_specs=[smem] * scalars + [vmem] * (len(operands) - scalars),
        out_specs=jax.tree.map(lambda _: vmem, out_shape),
        scratch_shapes=scratch,
        input_output_aliases=aliases,
        cost_estimate=pl.CostEstimate(flops=flops, transcendentals=0, bytes_accessed=2 * 10**6),
    )(*operands)


def chol_inverse(core, mine, other, n):
    scratch = [pltpu.VMEM(s, jnp.float32) for s in ((SIDE, n), (SIDE, SIDE), (SIDE, SIDE), (64, SIDE))]
    return call(chol_kernel, jax.ShapeDtypeStruct((n, n), jnp.float32), scratch, {}, 2 * 10**10, 1, core, mine, other)


def near_kernel(own_ref, points_ref, below_ref, above_ref, near_ref, turned_ref, spread_ref):
    rows, orbs = own_ref.shape
    middle = rows // 2
    tall = 2 * rows
    parts = [
        (0, rows, own_ref, points_ref, 0),
        (rows, middle, below_ref, below_ref, middle),
        (rows + middle, middle, above_ref, above_ref, middle),
    ]
    for start, size, ref, coords, first in parts:
        for at in range(0, size, middle):
            value = ref[at : at + middle, :]
            there = slice(start + at, start + at + middle)
            upper, lower = split(value)
            near_ref[there, :orbs] = upper
            near_ref[there, orbs : 2 * orbs] = upper
            near_ref[there, 2 * orbs :] = lower
            upper, lower = split(value.T)
            for place, half in enumerate((upper, upper, lower)):
                turned_ref[:, place * tall + start + at : place * tall + start + at + middle] = half
            for k in range(3):
                line = coords[first + k : first + k + 1, at : at + middle]
                spread_ref[k, there, :] = jnp.broadcast_to(line, (SIDE, middle)).T


def add_tile(near_ref, spread_ref, acc, out, pieces, wide_far, tall_far, slab):
    chunk = pieces[0].shape[0] - 8
    orbs = out.shape[1]
    width = len(pieces) * chunk
    lane = lax.broadcasted_iota(jnp.int32, (8, SIDE), 1)
    for number, piece in enumerate(pieces):
        upper, lower = split(piece[:chunk, :])
        here = slice(number * chunk, number * chunk + chunk)
        for place, half in enumerate((upper, lower, upper)):
            wide_far[here, place * orbs : place * orbs + orbs] = half
            tall_far[place * width + number * chunk : place * width + number * chunk + chunk, :] = half
    for number in range(0, len(pieces), 2):
        left, right = (pieces[number + i][chunk : chunk + 8, :SIDE] for i in range(2))
        at = number * chunk
        slab[:, at : at + SIDE] = jnp.where(lane < chunk, left, pltpu.roll(right, chunk, 1))
    step = out.shape[0]
    for index in range(out.shape[0] // step):
        here = slice(index * step, index * step + step)
        gram = dot(near_ref[here, :], wide_far[...], ((1,), (1,)), None)
        squares = []
        for at in range(0, width, SIDE):
            square = 0.0025
            for k in range(3):
                spacing = spread_ref[k, here, :] - slab[k : k + 1, at : at + SIDE]
                square = square + spacing * spacing
            squares.append(square)
        upper, lower = split(gram * lax.rsqrt(jnp.concatenate(squares, axis=1)))
        product = dot(jnp.concatenate([upper, upper, lower], axis=1), tall_far[...], ((1,), (0,)), None)
        out[here, :] = product if acc is None else acc[here, :] + product


def first_kernel(pieces, *refs):
    found, out, scratch = refs[2 : 2 + pieces], refs[2 + pieces], refs[3 + pieces :]
    add_tile(*refs[:2], None, out, found, *scratch)


def tile_kernel(pieces, *refs):
    acc, found, out, scratch = refs[2], refs[3 : 3 + pieces], refs[3 + pieces], refs[4 + pieces :]
    add_tile(*refs[:2], acc, out, found, *scratch)


def last_kernel(pieces, weight, core_ref, near_ref, spread_ref, turned_ref, acc, *refs):
    found = refs[:pieces]
    own_ref, below_ref, above_ref, mine_ref, other_ref, total, halves = refs[pieces : 7 + pieces]
    add_tile(near_ref, spread_ref, acc, total, found, *refs[7 + pieces :])
    rows = own_ref.shape[0]
    middle = rows // 2
    tall = 2 * rows
    own_ref[...] = total[:rows, :] * weight
    below_ref[...] = total[rows : rows + middle, :] * weight
    above_ref[...] = total[rows + middle :, :] * weight
    upper, lower = split(total[...])
    for place, half in enumerate((upper, lower, upper)):
        halves[place * tall : place * tall + tall, :] = half
    count = total.shape[1] // SIDE
    number = 0
    each = count * (count + 1) // 4
    for i in range(count):
        left = turned_ref[i * SIDE : i * SIDE + SIDE, :]
        wide = dot(left, halves[:, i * SIDE :], ((1,), (0,)), None) * (weight * weight)
        for j in range(i, count):
            block = wide[:, (j - i) * SIDE : (j - i) * SIDE + SIDE]
            there = slice(number % each * SIDE, number % each * SIDE + SIDE)

            @pl.when(core_ref[0] == number // each)
            def _():
                mine_ref[there, :] = block

            @pl.when(core_ref[0] != number // each)
            def _():
                other_ref[there, :] = block

            number += 1


def scratch(pieces, chunk, orbs):
    wide = pieces * chunk
    return [
        pltpu.VMEM((wide, 3 * orbs), jnp.bfloat16),
        pltpu.VMEM((3 * wide, orbs), jnp.bfloat16),
        pltpu.VMEM((8, wide), jnp.float32),
    ]


def shift(block, axis, distance):
    size = lax.axis_size(axis)
    return lax.ppermute(block, axis, [(i, (i + distance) % size) for i in range(size)])


def shift_y(block, distance):
    size = lax.axis_size(("yl", "yh"))
    place = [(y % 2) * (size // 2) + y // 2 for y in range(size)]
    return lax.ppermute(block, ("yl", "yh"), [(place[y], place[(y + distance) % size]) for y in range(size)])


def gathered(piece, axes):
    copies = jnp.broadcast_to(piece[None], (lax.axis_size(axes),) + piece.shape)
    return lax.all_to_all(copies, axes, 0, 0, tiled=True)


def scattered_sum(parts, axes):
    return jnp.sum(lax.all_to_all(parts, axes, 0, 0, tiled=True), axis=0)


def packed(rows, coords):
    return jnp.concatenate([rows, jnp.pad(coords, ((0, 5), (0, rows.shape[1] - coords.shape[1])))], axis=0)


def shards(orbitals, points):
    rows, orbs = orbitals.shape
    core = lax.axis_index("c")
    core_ref = core.astype(jnp.int32)[None]
    groups = lax.axis_size(("yh", "x"))
    group = lax.axis_index(("yh", "x"))
    chunk = rows // groups
    weight = 1.0 / (rows * lax.axis_size(("yl", "z", "c")))
    barrier = lax.optimization_barrier

    own = packed(
        lax.dynamic_slice_in_dim(orbitals, group * chunk, chunk, 0),
        lax.dynamic_slice_in_dim(points, group * chunk, chunk, 1),
    )
    middle = rows // 2
    from_below = shift_y(packed(orbitals[:middle], points[:, :middle]), 1)
    from_above = shift_y(packed(orbitals[middle:], points[:, middle:]), -1)
    far = {0: own}
    ring = lax.axis_size("z")
    order = [0]
    for distance in range(1, ring // 2):
        order += [distance, -distance]
    order.append(ring // 2)
    for distance in order[1:]:
        far[distance] = shift(own, "z", distance)

    tall = 2 * rows
    near_type = jax.ShapeDtypeStruct((tall, 3 * orbs), jnp.bfloat16)
    turned_type = jax.ShapeDtypeStruct((orbs, 3 * tall), jnp.bfloat16)
    spread_type = jax.ShapeDtypeStruct((3, tall, SIDE), jnp.float32)
    near, turned, spread = call(
        near_kernel, (near_type, turned_type, spread_type), [], {}, 10**9, 0, orbitals, points, from_below, from_above
    )
    total_type = jax.ShapeDtypeStruct((tall, orbs), jnp.float32)
    stages = [order[:3], order[3:5], order[5:7], order[7:]]
    total = None
    for number, stage in enumerate(stages):
        pieces = []
        for distance in stage:
            pieces += [far[distance], shift(far[distance], "c", 1)]
        count = len(pieces)
        if number == 0:
            body = functools.partial(first_kernel, count)
            total = call(body, total_type, scratch(count, chunk, orbs), {}, 4 * 10**9, 0, near, spread, *pieces)
        elif number < len(stages) - 1:
            body = functools.partial(tile_kernel, count)
            total = call(body, total_type, scratch(count, chunk, orbs), {2: 0}, 3 * 10**9, 0, near, spread, total, *pieces)
    tri = (orbs // SIDE) * (orbs // SIDE + 1) // 4 * SIDE
    middle_type = jax.ShapeDtypeStruct((middle, orbs), jnp.float32)
    tri_type = jax.ShapeDtypeStruct((tri, SIDE), jnp.float32)
    own_part, to_above, to_below, mine, other = call(
        functools.partial(last_kernel, count, weight),
        (jax.ShapeDtypeStruct((rows, orbs), jnp.float32), middle_type, middle_type, tri_type, tri_type),
        [pltpu.VMEM((tall, orbs), jnp.float32), pltpu.VMEM((3 * tall, orbs), jnp.bfloat16)] + scratch(count, chunk, orbs),
        {}, 3 * 10**9, 1, core_ref, near, spread, turned, total, *pieces,
    )

    half = mine + shift(other, "c", 1)
    to_above = shift_y(to_above, 1)
    to_below = shift_y(to_below, -1)
    plane = lax.axis_size(PLANE)
    piece = scattered_sum(half.reshape(plane, -1, SIDE), PLANE)
    piece, to_above, to_below = barrier((piece, to_above, to_below))

    applied = own_part + jnp.concatenate([to_above, to_below], axis=0)
    lines = lax.axis_size("x")
    line, yh = lax.axis_index("x"), lax.axis_index("yh")
    by_line = applied.reshape(groups // lines, lines, chunk, orbs)
    parts = [lax.dynamic_index_in_dim(by_line, line, 1, keepdims=False)]
    for distance in range(1, lines):
        part = lax.dynamic_index_in_dim(by_line, (line + distance) % lines, 1, keepdims=False)
        parts.append(shift(part, "x", distance))
    piece = jnp.sum(gathered(piece, "z"), axis=0)
    pair = sum(parts[1:], parts[0])
    kept = lax.dynamic_index_in_dim(pair, yh, 0, keepdims=False)
    sent = shift(lax.dynamic_index_in_dim(pair, 1 - yh, 0, keepdims=False), "yh", 1)

    half = gathered(piece, PLANE).reshape(-1, SIDE)
    half, kept, sent = barrier((half, kept, sent))
    applied = kept + sent
    far_half, applied = barrier((shift(half, "c", 1), applied))
    applied = gathered(applied, ("yh", "x")).reshape(rows, orbs)
    inverse = chol_inverse(core_ref, half, far_half, orbs)
    return -dot(applied, inverse, ((1,), (1,)))


def solution(mesh):
    fine = Mesh(mesh.devices.reshape(2, 8, 2, 2, 4), ("yl", "z", "c", "yh", "x"))
    blk = ("yl", "z", "c")

    return jax.shard_map(
        shards,
        mesh=fine,
        in_specs=(P(blk, None), P(None, blk)),
        out_specs=P(blk, None),
        check_vma=False,
    )
```

```python
import functools

import jax
import jax.numpy as jnp
from jax import lax
from jax.experimental import pallas as pl
from jax.experimental.pallas import tpu as pltpu
from jax.sharding import Mesh, PartitionSpec as P


HIGHEST = lax.Precision.HIGHEST
PLANE = ("x", "yh", "yl")

SIDE = 128


def lanes(value, index):
    return jnp.broadcast_to(value[:, index : index + 1], (8, SIDE))


def base(a_ref, z_ref, spread):
    strips = SIDE // 8
    lane = lax.broadcasted_iota(jnp.int32, (8, SIDE), 1)

    def opened(strip, block):
        start = 8 * strip
        inside = (lane >= start) & (lane < start + 8)
        for k in range(8):
            spread[8 * k : 8 * k + 8, :] = lanes(block, start + k)
        p = [[None] * 8 for _ in range(8)]
        for i in range(8):
            for k in range(i + 1):
                p[i][k] = p[k][i] = jnp.broadcast_to(spread[8 * k + i : 8 * k + i + 1, :], (8, SIDE))
        row = [jnp.broadcast_to(a_ref[start + i : start + i + 1, :], (8, SIDE)) for i in range(8)]
        row = [jnp.where(inside, jnp.where(lane == start + i, 1.0, 0.0), row[i]) for i in range(8)]
        return start, inside, row, p

    def update(strip, later, inside, row):
        there = slice(8 * later, 8 * later + 8)
        block = a_ref[there, :]
        product = [lanes(block, 8 * strip + k) * row[k] for k in range(8)]
        while len(product) > 1:
            product = [product[i] + product[i + 1] for i in range(0, len(product), 2)]
        block = jnp.where(inside, 0.0, block) - product[0]
        a_ref[there, :] = block
        return block

    state = opened(0, a_ref[:8, :])
    for strip in range(strips):
        start, inside, row, p = state
        for k in range(8):
            inv = 1.0 / p[k][k]
            z_ref[start + k : start + k + 1, :] = (row[k] * lax.rsqrt(p[k][k]))[:1]
            scaled = [None if i == k else p[i][k] * inv for i in range(8)]
            for i in list(range(k + 1, 8)) + list(range(k)):
                for l in range(k + 1, 8):
                    if i > k and l > i:
                        continue
                    if i == l == k + 1:
                        p[i][l] = p[i][l] - (p[i][k] * p[k][l]) * inv
                    else:
                        p[i][l] = p[i][l] - scaled[i] * p[k][l]
                    if i > k:
                        p[l][i] = p[i][l]
            for l in range(k + 1, 8):
                p[k][l] = scaled[l] if l > k else p[k][l]
            for i in range(8):
                if i != k:
                    row[i] = row[i] - scaled[i] * row[k]
            row[k] = row[k] * inv
        if strip + 1 < strips:
            state = opened(strip + 1, update(strip, strip + 1, inside, row))
        for later in range(strip + 2, strips):
            update(strip, later, inside, row)


def dot(a, b, dims, precision=HIGHEST):
    return lax.dot_general(a, b, (dims, ((), ())), precision=precision, preferred_element_type=jnp.float32)


def split(value):
    upper = value.astype(jnp.bfloat16)
    return upper, (value - upper.astype(jnp.float32)).astype(jnp.bfloat16)


def chol_kernel(core_ref, mine_ref, other_ref, z_ref, rows, base_a, base_z, spread):
    n = z_ref.shape[0]
    count = n // SIDE
    where = [(i, j) for i in range(count) for j in range(i, count)]
    each = len(where) // 2
    for number, (i, j) in enumerate(where):
        here = slice(number % each * SIDE, number % each * SIDE + SIDE)
        block = jnp.where(core_ref[0] == number // each, mine_ref[here, :], other_ref[here, :])
        z_ref[i * SIDE : i * SIDE + SIDE, j * SIDE : j * SIDE + SIDE] = block
        if i < j:
            z_ref[j * SIDE : j * SIDE + SIDE, i * SIDE : i * SIDE + SIDE] = jnp.zeros((SIDE, SIDE), jnp.float32)
    row = lax.broadcasted_iota(jnp.int32, (SIDE, SIDE), 0)
    column = lax.broadcasted_iota(jnp.int32, (SIDE, SIDE), 1)
    eye = jnp.where(row == column, 1.0, 0.0)

    def step(index, carry):
        here = pl.ds(pl.multiple_of(index * SIDE, SIDE), SIDE)
        base_a[...] = z_ref[here, here]
        base(base_a, base_z, spread)
        z_ref[here, here] = eye
        lower = jnp.where(row >= column, base_z[...], 0.0)
        rows[...] = dot(lower, z_ref[here, :], ((1,), (0,)))
        z_ref[here, :] = rows[...]

        def update(later, inner):
            there = pl.ds(pl.multiple_of(later * SIDE, SIDE), SIDE)
            z_ref[there, here] = jnp.zeros((SIDE, SIDE), jnp.float32)
            z_ref[there, :] = z_ref[there, :] - dot(rows[:, there], rows[...], ((0,), (0,)))
            return inner

        lax.fori_loop(index + 1, count, update, 0)
        return carry

    lax.fori_loop(0, count, step, 0)
    for i in range(count):
        for j in range(i + 1, count):
            z_ref[i * SIDE : i * SIDE + SIDE, j * SIDE : j * SIDE + SIDE] = jnp.zeros((SIDE, SIDE), jnp.float32)


def call(body, out_shape, scratch, aliases, flops, scalars, *operands):
    vmem = pl.BlockSpec(memory_space=pltpu.VMEM)
    smem = pl.BlockSpec(memory_space=pltpu.SMEM)
    return pl.pallas_call(
        body,
        out_shape=out_shape,
        in_specs=[smem] * scalars + [vmem] * (len(operands) - scalars),
        out_specs=jax.tree.map(lambda _: vmem, out_shape),
        scratch_shapes=scratch,
        input_output_aliases=aliases,
        cost_estimate=pl.CostEstimate(flops=flops, transcendentals=0, bytes_accessed=2 * 10**6),
        compiler_params=pltpu.CompilerParams(vmem_limit_bytes=16 * 2**20),
    )(*operands)


def chol_inverse(core, mine, other, n):
    scratch = [pltpu.VMEM(s, jnp.float32) for s in ((SIDE, n), (SIDE, SIDE), (SIDE, SIDE), (64, SIDE))]
    return call(chol_kernel, jax.ShapeDtypeStruct((n, n), jnp.float32), scratch, {}, 2 * 10**10, 1, core, mine, other)


def near_kernel(core_ref, line_ref, yh_ref, own_ref, points_ref, below_ref, above_ref, near_ref, turned_ref, spread_ref):
    rows, orbs = own_ref.shape
    middle = rows // 2
    tall = 2 * rows
    parts = [
        (0, rows, own_ref, points_ref, 0),
        (rows, middle, below_ref, below_ref, middle),
        (rows + middle, middle, above_ref, above_ref, middle),
    ]
    for start, size, ref, coords, first in parts:
        for at in range(0, size, middle):
            value = ref[at : at + middle, :]
            there = slice(start + at, start + at + middle)
            upper, lower = split(value)
            near_ref[there, :orbs] = upper
            near_ref[there, orbs : 2 * orbs] = upper
            near_ref[there, 2 * orbs :] = lower
            upper, lower = split(value.T)
            for place, half in enumerate((upper, upper, lower)):
                turned_ref[:, place * tall + start + at : place * tall + start + at + middle] = half
            for k in range(3):
                line = coords[first + k : first + k + 1, at : at + middle]
                spread_ref[k, there, :] = jnp.broadcast_to(line, (SIDE, middle)).T


def add_tile(near_ref, spread_ref, acc, out, pieces, wide_far, tall_far, slab):
    chunk = pieces[0].shape[0] - 8
    orbs = out.shape[1]
    width = len(pieces) * chunk
    lane = lax.broadcasted_iota(jnp.int32, (8, SIDE), 1)
    for number, piece in enumerate(pieces):
        upper, lower = split(piece[:chunk, :])
        here = slice(number * chunk, number * chunk + chunk)
        for place, half in enumerate((upper, lower, upper)):
            wide_far[here, place * orbs : place * orbs + orbs] = half
            tall_far[place * width + number * chunk : place * width + number * chunk + chunk, :] = half
    for number in range(0, len(pieces), 2):
        left, right = (pieces[number + i][chunk : chunk + 8, :SIDE] for i in range(2))
        at = number * chunk
        slab[:, at : at + SIDE] = jnp.where(lane < chunk, left, pltpu.roll(right, chunk, 1))
    step = out.shape[0]
    for index in range(out.shape[0] // step):
        here = slice(index * step, index * step + step)
        gram = dot(near_ref[here, :], wide_far[...], ((1,), (1,)), None)
        squares = []
        for at in range(0, width, SIDE):
            square = 0.0025
            for k in range(3):
                spacing = spread_ref[k, here, :] - slab[k : k + 1, at : at + SIDE]
                square = square + spacing * spacing
            squares.append(square)
        upper, lower = split(gram * lax.rsqrt(jnp.concatenate(squares, axis=1)))
        product = dot(jnp.concatenate([upper, upper, lower], axis=1), tall_far[...], ((1,), (0,)), None)
        out[here, :] = product if acc is None else acc[here, :] + product


def first_kernel(pieces, *refs):
    found, out, scratch = refs[2 : 2 + pieces], refs[2 + pieces], refs[3 + pieces :]
    add_tile(*refs[:2], None, out, found, *scratch)


def tile_kernel(pieces, *refs):
    acc, found, out, scratch = refs[2], refs[3 : 3 + pieces], refs[3 + pieces], refs[4 + pieces :]
    add_tile(*refs[:2], acc, out, found, *scratch)


def last_kernel(pieces, weight, core_ref, near_ref, spread_ref, turned_ref, acc, *refs):
    found = refs[:pieces]
    own_ref, below_ref, above_ref, mine_ref, other_ref, total, halves = refs[pieces : 7 + pieces]
    add_tile(near_ref, spread_ref, acc, total, found, *refs[7 + pieces :])
    rows = own_ref.shape[0]
    middle = rows // 2
    tall = 2 * rows
    own_ref[...] = total[:rows, :] * weight
    below_ref[...] = total[rows : rows + middle, :] * weight
    above_ref[...] = total[rows + middle :, :] * weight
    upper, lower = split(total[...])
    for place, half in enumerate((upper, lower, upper)):
        halves[place * tall : place * tall + tall, :] = half
    count = total.shape[1] // SIDE
    number = 0
    each = count * (count + 1) // 4
    for i in range(count):
        left = turned_ref[i * SIDE : i * SIDE + SIDE, :]
        wide = dot(left, halves[:, i * SIDE :], ((1,), (0,)), None) * (weight * weight)
        for j in range(i, count):
            block = wide[:, (j - i) * SIDE : (j - i) * SIDE + SIDE]
            there = slice(number % each * SIDE, number % each * SIDE + SIDE)

            @pl.when(core_ref[0] == number // each)
            def _():
                mine_ref[there, :] = block

            @pl.when(core_ref[0] != number // each)
            def _():
                other_ref[there, :] = block

            number += 1


def scratch(pieces, chunk, orbs):
    wide = pieces * chunk
    return [
        pltpu.VMEM((wide, 3 * orbs), jnp.bfloat16),
        pltpu.VMEM((3 * wide, orbs), jnp.bfloat16),
        pltpu.VMEM((8, wide), jnp.float32),
    ]


def shift(block, axis, distance):
    size = lax.axis_size(axis)
    return lax.ppermute(block, axis, [(i, (i + distance) % size) for i in range(size)])


def shift_y(block, distance):
    size = lax.axis_size(("yl", "yh"))
    place = [(y % 2) * (size // 2) + y // 2 for y in range(size)]
    return lax.ppermute(block, ("yl", "yh"), [(place[y], place[(y + distance) % size]) for y in range(size)])


def gathered(piece, axes):
    copies = jnp.broadcast_to(piece[None], (lax.axis_size(axes),) + piece.shape)
    return lax.all_to_all(copies, axes, 0, 0, tiled=True)


def scattered_sum(parts, axes):
    return jnp.sum(lax.all_to_all(parts, axes, 0, 0, tiled=True), axis=0)


def packed(rows, coords):
    return jnp.concatenate([rows, jnp.pad(coords, ((0, 5), (0, rows.shape[1] - coords.shape[1])))], axis=0)


def shards(orbitals, points):
    rows, orbs = orbitals.shape
    core = lax.axis_index("c")
    line, yh = lax.axis_index("x"), lax.axis_index("yh")
    core_ref = core.astype(jnp.int32)[None]
    place = [core_ref, line.astype(jnp.int32)[None], yh.astype(jnp.int32)[None]]
    groups = lax.axis_size(("yh", "x"))
    group = lax.axis_index(("yh", "x"))
    chunk = rows // groups
    weight = 1.0 / (rows * lax.axis_size(("yl", "z", "c")))
    barrier = lax.optimization_barrier

    own = packed(
        lax.dynamic_slice_in_dim(orbitals, group * chunk, chunk, 0),
        lax.dynamic_slice_in_dim(points, group * chunk, chunk, 1),
    )
    middle = rows // 2
    from_below = shift_y(packed(orbitals[:middle], points[:, :middle]), 1)
    from_above = shift_y(packed(orbitals[middle:], points[:, middle:]), -1)
    far = {0: own}
    ring = lax.axis_size("z")
    order = [0]
    for distance in range(1, ring // 2):
        order += [distance, -distance]
    order.append(ring // 2)
    for distance in order[1:]:
        far[distance] = shift(own, "z", distance)

    tall = 2 * rows
    near_type = jax.ShapeDtypeStruct((tall, 3 * orbs), jnp.bfloat16)
    turned_type = jax.ShapeDtypeStruct((orbs, 3 * tall), jnp.bfloat16)
    spread_type = jax.ShapeDtypeStruct((3, tall, SIDE), jnp.float32)
    near, turned, spread = call(
        near_kernel, (near_type, turned_type, spread_type), [], {}, 10**9, 3, *place, orbitals, points, from_below, from_above
    )
    total_type = jax.ShapeDtypeStruct((tall, orbs), jnp.float32)
    stages = [order[:3], order[3:5], order[5:7], order[7:]]
    total = None
    for number, stage in enumerate(stages):
        pieces = []
        for distance in stage:
            pieces += [far[distance], shift(far[distance], "c", 1)]
        count = len(pieces)
        if number == 0:
            body = functools.partial(first_kernel, count)
            total = call(body, total_type, scratch(count, chunk, orbs), {}, 4 * 10**9, 0, near, spread, *pieces)
        elif number < len(stages) - 1:
            body = functools.partial(tile_kernel, count)
            total = call(body, total_type, scratch(count, chunk, orbs), {2: 0}, 3 * 10**9, 0, near, spread, total, *pieces)
    tri = (orbs // SIDE) * (orbs // SIDE + 1) // 4 * SIDE
    middle_type = jax.ShapeDtypeStruct((middle, orbs), jnp.float32)
    tri_type = jax.ShapeDtypeStruct((tri, SIDE), jnp.float32)
    own_part, to_above, to_below, mine, other = call(
        functools.partial(last_kernel, count, weight),
        (jax.ShapeDtypeStruct((rows, orbs), jnp.float32), middle_type, middle_type, tri_type, tri_type),
        [pltpu.VMEM((tall, orbs), jnp.float32), pltpu.VMEM((3 * tall, orbs), jnp.bfloat16)] + scratch(count, chunk, orbs),
        {}, 3 * 10**9, 1, core_ref, near, spread, turned, total, *pieces,
    )

    half = mine + shift(other, "c", 1)
    to_above = shift_y(to_above, 1)
    to_below = shift_y(to_below, -1)
    plane = lax.axis_size(PLANE)
    piece = scattered_sum(half.reshape(plane, -1, SIDE), PLANE)
    piece, to_above, to_below = barrier((piece, to_above, to_below))

    applied = own_part + jnp.concatenate([to_above, to_below], axis=0)
    lines = lax.axis_size("x")
    by_line = applied.reshape(groups // lines, lines, chunk, orbs)
    parts = [lax.dynamic_index_in_dim(by_line, line, 1, keepdims=False)]
    for distance in range(1, lines):
        part = lax.dynamic_index_in_dim(by_line, (line + distance) % lines, 1, keepdims=False)
        parts.append(shift(part, "x", distance))
    piece = jnp.sum(gathered(piece, "z"), axis=0)
    pair = sum(parts[1:], parts[0])
    kept = lax.dynamic_index_in_dim(pair, yh, 0, keepdims=False)
    sent = shift(lax.dynamic_index_in_dim(pair, 1 - yh, 0, keepdims=False), "yh", 1)

    half = gathered(piece, PLANE).reshape(-1, SIDE)
    half, kept, sent = barrier((half, kept, sent))
    applied = kept + sent
    far_half, applied = barrier((shift(half, "c", 1), applied))
    applied = gathered(applied, ("yh", "x")).reshape(rows, orbs)
    inverse = chol_inverse(core_ref, half, far_half, orbs)
    return -dot(applied, inverse, ((1,), (1,)))


def solution(mesh):
    fine = Mesh(mesh.devices.reshape(2, 8, 2, 2, 4), ("yl", "z", "c", "yh", "x"))
    blk = ("yl", "z", "c")

    return jax.shard_map(
        shards,
        mesh=fine,
        in_specs=(P(blk, None), P(None, blk)),
        out_specs=P(blk, None),
        check_vma=False,
    )
```

```python
import functools

import jax
import jax.numpy as jnp
from jax import lax
from jax.experimental import pallas as pl
from jax.experimental.pallas import tpu as pltpu
from jax.sharding import Mesh, PartitionSpec as P


HIGHEST = lax.Precision.HIGHEST
PLANE = ("x", "yh", "yl")

SIDE = 128


def lanes(value, index):
    return jnp.broadcast_to(value[:, index : index + 1], (8, SIDE))


def base(a_ref, z_ref, spread):
    strips = SIDE // 8
    lane = lax.broadcasted_iota(jnp.int32, (8, SIDE), 1)

    def opened(strip, block):
        start = 8 * strip
        inside = (lane >= start) & (lane < start + 8)
        for k in range(8):
            spread[8 * k : 8 * k + 8, :] = lanes(block, start + k)
        p = [[None] * 8 for _ in range(8)]
        for i in range(8):
            for k in range(i + 1):
                p[i][k] = p[k][i] = jnp.broadcast_to(spread[8 * k + i : 8 * k + i + 1, :], (8, SIDE))
        row = [jnp.broadcast_to(a_ref[start + i : start + i + 1, :], (8, SIDE)) for i in range(8)]
        row = [jnp.where(inside, jnp.where(lane == start + i, 1.0, 0.0), row[i]) for i in range(8)]
        return start, inside, row, p

    def update(strip, later, inside, row):
        there = slice(8 * later, 8 * later + 8)
        block = a_ref[there, :]
        product = [lanes(block, 8 * strip + k) * row[k] for k in range(8)]
        while len(product) > 1:
            product = [product[i] + product[i + 1] for i in range(0, len(product), 2)]
        block = jnp.where(inside, 0.0, block) - product[0]
        a_ref[there, :] = block
        return block

    state = opened(0, a_ref[:8, :])
    for strip in range(strips):
        start, inside, row, p = state
        for k in range(8):
            inv = 1.0 / p[k][k]
            z_ref[start + k : start + k + 1, :] = (row[k] * lax.rsqrt(p[k][k]))[:1]
            scaled = [None if i == k else p[i][k] * inv for i in range(8)]
            for i in list(range(k + 1, 8)) + list(range(k)):
                for l in range(k + 1, 8):
                    if i > k and l > i:
                        continue
                    if i == l == k + 1:
                        p[i][l] = p[i][l] - (p[i][k] * p[k][l]) * inv
                    else:
                        p[i][l] = p[i][l] - scaled[i] * p[k][l]
                    if i > k:
                        p[l][i] = p[i][l]
            for l in range(k + 1, 8):
                p[k][l] = scaled[l] if l > k else p[k][l]
            for i in range(8):
                if i != k:
                    row[i] = row[i] - scaled[i] * row[k]
            row[k] = row[k] * inv
        if strip + 1 < strips:
            state = opened(strip + 1, update(strip, strip + 1, inside, row))
        for later in range(strip + 2, strips):
            update(strip, later, inside, row)


def dot(a, b, dims, precision=HIGHEST):
    return lax.dot_general(a, b, (dims, ((), ())), precision=precision, preferred_element_type=jnp.float32)


def split(value):
    upper = value.astype(jnp.bfloat16)
    return upper, (value - upper.astype(jnp.float32)).astype(jnp.bfloat16)


def chol_kernel(core_ref, mine_ref, other_ref, z_ref, rows, base_a, base_z, spread):
    n = z_ref.shape[0]
    count = n // SIDE
    where = [(i, j) for i in range(count) for j in range(i, count)]
    each = len(where) // 2
    for number, (i, j) in enumerate(where):
        here = slice(number % each * SIDE, number % each * SIDE + SIDE)
        block = jnp.where(core_ref[0] == number // each, mine_ref[here, :], other_ref[here, :])
        z_ref[i * SIDE : i * SIDE + SIDE, j * SIDE : j * SIDE + SIDE] = block
        if i < j:
            z_ref[j * SIDE : j * SIDE + SIDE, i * SIDE : i * SIDE + SIDE] = jnp.zeros((SIDE, SIDE), jnp.float32)
    row = lax.broadcasted_iota(jnp.int32, (SIDE, SIDE), 0)
    column = lax.broadcasted_iota(jnp.int32, (SIDE, SIDE), 1)
    eye = jnp.where(row == column, 1.0, 0.0)

    def step(index, carry):
        here = pl.ds(pl.multiple_of(index * SIDE, SIDE), SIDE)
        base_a[...] = z_ref[here, here]
        base(base_a, base_z, spread)
        z_ref[here, here] = eye
        lower = jnp.where(row >= column, base_z[...], 0.0)
        rows[...] = dot(lower, z_ref[here, :], ((1,), (0,)))
        z_ref[here, :] = rows[...]

        def update(later, inner):
            there = pl.ds(pl.multiple_of(later * SIDE, SIDE), SIDE)
            z_ref[there, here] = jnp.zeros((SIDE, SIDE), jnp.float32)
            z_ref[there, :] = z_ref[there, :] - dot(rows[:, there], rows[...], ((0,), (0,)))
            return inner

        lax.fori_loop(index + 1, count, update, 0)
        return carry

    lax.fori_loop(0, count, step, 0)
    for i in range(count):
        for j in range(i + 1, count):
            z_ref[i * SIDE : i * SIDE + SIDE, j * SIDE : j * SIDE + SIDE] = jnp.zeros((SIDE, SIDE), jnp.float32)


def call(body, out_shape, scratch, aliases, flops, scalars, *operands):
    vmem = pl.BlockSpec(memory_space=pltpu.VMEM)
    smem = pl.BlockSpec(memory_space=pltpu.SMEM)
    return pl.pallas_call(
        body,
        out_shape=out_shape,
        in_specs=[smem] * scalars + [vmem] * (len(operands) - scalars),
        out_specs=jax.tree.map(lambda _: vmem, out_shape),
        scratch_shapes=scratch,
        input_output_aliases=aliases,
        cost_estimate=pl.CostEstimate(flops=flops, transcendentals=0, bytes_accessed=2 * 10**6),
        compiler_params=pltpu.CompilerParams(vmem_limit_bytes=16 * 2**20),
    )(*operands)


def chol_inverse(core, mine, other, n):
    scratch = [pltpu.VMEM(s, jnp.float32) for s in ((SIDE, n), (SIDE, SIDE), (SIDE, SIDE), (64, SIDE))]
    return call(chol_kernel, jax.ShapeDtypeStruct((n, n), jnp.float32), scratch, {}, 2 * 10**10, 1, core, mine, other)


def near_kernel(lower_ref, upper_ref, below_ref, above_ref, near_ref, turned_ref, spread_ref):
    middle, orbs = lower_ref.shape[0] - 8, lower_ref.shape[1]
    tall = near_ref.shape[0]
    for part, ref in enumerate((lower_ref, upper_ref, below_ref, above_ref)):
        there = slice(part * middle, part * middle + middle)
        value = ref[:middle, :]
        upper, lower = split(value)
        near_ref[there, :orbs] = upper
        near_ref[there, orbs : 2 * orbs] = upper
        near_ref[there, 2 * orbs :] = lower
        upper, lower = split(value.T)
        for place, half in enumerate((upper, upper, lower)):
            turned_ref[:, place * tall + part * middle : place * tall + part * middle + middle] = half
        for k in range(3):
            line = ref[middle + k : middle + k + 1, :middle]
            spread_ref[k, there, :] = jnp.broadcast_to(line, (SIDE, middle)).T


def add_tile(near_ref, spread_ref, acc, out, pieces, wide_far, tall_far, slab):
    chunk = pieces[0].shape[0] - 8
    orbs = out.shape[1]
    width = len(pieces) * chunk
    lane = lax.broadcasted_iota(jnp.int32, (8, SIDE), 1)
    for number, piece in enumerate(pieces):
        upper, lower = split(piece[:chunk, :])
        here = slice(number * chunk, number * chunk + chunk)
        for place, half in enumerate((upper, lower, upper)):
            wide_far[here, place * orbs : place * orbs + orbs] = half
            tall_far[place * width + number * chunk : place * width + number * chunk + chunk, :] = half
    for number in range(0, len(pieces), 2):
        left, right = (pieces[number + i][chunk : chunk + 8, :SIDE] for i in range(2))
        at = number * chunk
        slab[:, at : at + SIDE] = jnp.where(lane < chunk, left, pltpu.roll(right, chunk, 1))
    step = out.shape[0]
    for index in range(out.shape[0] // step):
        here = slice(index * step, index * step + step)
        gram = dot(near_ref[here, :], wide_far[...], ((1,), (1,)), None)
        squares = []
        for at in range(0, width, SIDE):
            square = 0.0025
            for k in range(3):
                spacing = spread_ref[k, here, :] - slab[k : k + 1, at : at + SIDE]
                square = square + spacing * spacing
            squares.append(square)
        upper, lower = split(gram * lax.rsqrt(jnp.concatenate(squares, axis=1)))
        product = dot(jnp.concatenate([upper, upper, lower], axis=1), tall_far[...], ((1,), (0,)), None)
        out[here, :] = product if acc is None else acc[here, :] + product


def first_kernel(pieces, *refs):
    found, out, scratch = refs[2 : 2 + pieces], refs[2 + pieces], refs[3 + pieces :]
    add_tile(*refs[:2], None, out, found, *scratch)


def tile_kernel(pieces, *refs):
    acc, found, out, scratch = refs[2], refs[3 : 3 + pieces], refs[3 + pieces], refs[4 + pieces :]
    add_tile(*refs[:2], acc, out, found, *scratch)


def last_kernel(pieces, weight, core_ref, near_ref, spread_ref, turned_ref, acc, *refs):
    found = refs[:pieces]
    own_ref, below_ref, above_ref, mine_ref, other_ref, total, halves = refs[pieces : 7 + pieces]
    add_tile(near_ref, spread_ref, acc, total, found, *refs[7 + pieces :])
    rows = own_ref.shape[0]
    middle = rows // 2
    tall = 2 * rows
    own_ref[...] = total[:rows, :] * weight
    below_ref[...] = total[rows : rows + middle, :] * weight
    above_ref[...] = total[rows + middle :, :] * weight
    upper, lower = split(total[...])
    for place, half in enumerate((upper, lower, upper)):
        halves[place * tall : place * tall + tall, :] = half
    count = total.shape[1] // SIDE
    number = 0
    each = count * (count + 1) // 4
    for i in range(count):
        left = turned_ref[i * SIDE : i * SIDE + SIDE, :]
        wide = dot(left, halves[:, i * SIDE :], ((1,), (0,)), None) * (weight * weight)
        for j in range(i, count):
            block = wide[:, (j - i) * SIDE : (j - i) * SIDE + SIDE]
            there = slice(number % each * SIDE, number % each * SIDE + SIDE)

            @pl.when(core_ref[0] == number // each)
            def _():
                mine_ref[there, :] = block

            @pl.when(core_ref[0] != number // each)
            def _():
                other_ref[there, :] = block

            number += 1


def pack_kernel(group_ref, core_ref, line_ref, rows_ref, points_ref, own_ref, below_ref, above_ref):
    chunk = own_ref.shape[0] - 8
    rows, orbs = rows_ref.shape
    middle = rows // 2
    own_ref[:chunk, :] = rows_ref[pl.ds(pl.multiple_of(group_ref[0] * chunk, chunk), chunk), :]
    for line in range(3):
        turned = pltpu.roll(jnp.broadcast_to(points_ref[line : line + 1, :], (8, rows)), rows - group_ref[0] * chunk, 1)
        own_ref[chunk + line : chunk + line + 1, :] = turned[:1, :orbs]
    own_ref[chunk + 3 :, :] = jnp.zeros((5, orbs), jnp.float32)
    for start, ref in ((0, below_ref), (middle, above_ref)):
        ref[:middle, :] = rows_ref[start : start + middle, :]
        ref[middle:, :] = jnp.zeros((8, orbs), jnp.float32)
        ref[middle : middle + 3, :middle] = points_ref[:, start : start + middle]


def mark_kernel(number_ref, out_ref):
    out_ref[0] = number_ref[0]


def mark(number):
    smem = pl.BlockSpec(memory_space=pltpu.SMEM)
    out_shape = jax.ShapeDtypeStruct((1,), jnp.int32)
    params = pltpu.CompilerParams(vmem_limit_bytes=2**20)
    return pl.pallas_call(mark_kernel, out_shape=out_shape, in_specs=[smem], out_specs=smem, compiler_params=params)(number)


def final_kernel(line_ref, *refs):
    pieces, inverse_ref, out_ref, joined = refs[:-3], refs[-3], refs[-2], refs[-1]
    lines, halves, chunk = len(pieces), pieces[0].shape[0], pieces[0].shape[1]
    for number, piece in enumerate(pieces):
        for half in range(halves):
            at = (number * halves + half) * chunk
            joined[at : at + chunk, :] = piece[half]

    def block(pair, carry):
        start = pl.multiple_of(pair * 2 * halves * chunk, 2 * halves * chunk)
        product = dot(joined[pl.ds(start, 2 * halves * chunk), :], inverse_ref[...], ((1,), (1,)))
        for step in range(2):
            sender = (line_ref[0] + (lines - 2 * pair - step)) % lines
            for half in range(halves):
                at = (step * halves + half) * chunk
                there = pl.ds(pl.multiple_of((half * lines + sender) * chunk, chunk), chunk)
                out_ref[there, :] = -product[at : at + chunk, :]
        return carry

    lax.fori_loop(0, lines // 2, block, 0)


def scratch(pieces, chunk, orbs):
    wide = pieces * chunk
    return [
        pltpu.VMEM((wide, 3 * orbs), jnp.bfloat16),
        pltpu.VMEM((3 * wide, orbs), jnp.bfloat16),
        pltpu.VMEM((8, wide), jnp.float32),
    ]


def shift(block, axis, distance):
    size = lax.axis_size(axis)
    return lax.ppermute(block, axis, [(i, (i + distance) % size) for i in range(size)])


def shift_y(block, distance):
    size = lax.axis_size(("yl", "yh"))
    place = [(y % 2) * (size // 2) + y // 2 for y in range(size)]
    return lax.ppermute(block, ("yl", "yh"), [(place[y], place[(y + distance) % size]) for y in range(size)])


def gathered(piece, axes):
    copies = jnp.broadcast_to(piece[None], (lax.axis_size(axes),) + piece.shape)
    return lax.all_to_all(copies, axes, 0, 0, tiled=True)


def scattered_sum(parts, axes):
    return jnp.sum(lax.all_to_all(parts, axes, 0, 0, tiled=True), axis=0)


def shards(orbitals, points):
    rows, orbs = orbitals.shape
    core = lax.axis_index("c")
    line = lax.axis_index("x")
    core_ref = core.astype(jnp.int32)[None]
    place = [core_ref, line.astype(jnp.int32)[None]]
    groups = lax.axis_size(("yh", "x"))
    group = lax.axis_index(("yh", "x"))
    chunk = rows // groups
    weight = 1.0 / (rows * lax.axis_size(("yl", "z", "c")))

    middle = rows // 2
    message = [jax.ShapeDtypeStruct((size + 8, orbs), jnp.float32) for size in (chunk, middle, middle)]
    group_ref = group.astype(jnp.int32)[None]
    own, lower_half, upper_half = call(pack_kernel, tuple(message), [], {}, 10**8, 3, group_ref, *place, orbitals, points)
    from_below = shift_y(lower_half, 1)
    from_above = shift_y(upper_half, -1)
    far = {0: own}
    ring = lax.axis_size("z")
    order = [0]
    for distance in range(1, ring // 2):
        order += [distance, -distance]
    order.append(ring // 2)
    for distance in order[1:]:
        far[distance] = shift(own, "z", distance)

    tall = 2 * rows
    near_type = jax.ShapeDtypeStruct((tall, 3 * orbs), jnp.bfloat16)
    turned_type = jax.ShapeDtypeStruct((orbs, 3 * tall), jnp.bfloat16)
    spread_type = jax.ShapeDtypeStruct((3, tall, SIDE), jnp.float32)
    near, turned, spread = call(
        near_kernel, (near_type, turned_type, spread_type), [], {}, 10**9, 0, lower_half, upper_half, from_below, from_above
    )
    total_type = jax.ShapeDtypeStruct((tall, orbs), jnp.float32)
    stages = [order[:3], order[3:5], order[5:7], order[7:]]
    total = None
    for number, stage in enumerate(stages):
        pieces = []
        for distance in stage:
            pieces += [far[distance], shift(far[distance], "c", 1)]
        count = len(pieces)
        if number == 0:
            body = functools.partial(first_kernel, count)
            total = call(body, total_type, scratch(count, chunk, orbs), {}, 4 * 10**9, 0, near, spread, *pieces)
        elif number < len(stages) - 1:
            body = functools.partial(tile_kernel, count)
            total = call(body, total_type, scratch(count, chunk, orbs), {2: 0}, 3 * 10**9, 0, near, spread, total, *pieces)
    tri = (orbs // SIDE) * (orbs // SIDE + 1) // 4 * SIDE
    middle_type = jax.ShapeDtypeStruct((middle, orbs), jnp.float32)
    tri_type = jax.ShapeDtypeStruct((tri, SIDE), jnp.float32)
    own_part, to_above, to_below, mine, other = call(
        functools.partial(last_kernel, count, weight),
        (jax.ShapeDtypeStruct((rows, orbs), jnp.float32), middle_type, middle_type, tri_type, tri_type),
        [pltpu.VMEM((tall, orbs), jnp.float32), pltpu.VMEM((3 * tall, orbs), jnp.bfloat16)] + scratch(count, chunk, orbs),
        {}, 3 * 10**9, 1, core_ref, near, spread, turned, total, *pieces,
    )

    half = mine + shift(other, "c", 1)
    to_above = shift_y(to_above, 1)
    to_below = shift_y(to_below, -1)
    plane = lax.axis_size(PLANE)
    piece = scattered_sum(half.reshape(plane, -1, SIDE), PLANE)
    applied = own_part + jnp.concatenate([to_above, to_below], axis=0)
    lines = lax.axis_size("x")
    by_line = applied.reshape(groups // lines, lines, chunk, orbs)
    parts = [lax.dynamic_index_in_dim(by_line, line, 1, keepdims=False)]
    for distance in range(1, lines):
        part = lax.dynamic_index_in_dim(by_line, (line + distance) % lines, 1, keepdims=False)
        parts.append(shift(part, "x", distance))
    piece = jnp.sum(gathered(piece, "z"), axis=0)
    pair = sum(parts[1:], parts[0])
    other_pair = shift(pair, "yh", 1)
    half = gathered(piece, PLANE).reshape(-1, SIDE)
    pair = pair + other_pair
    held = [pair]
    for distance in range(1, lines):
        held.append(shift(pair, "x", distance))
    line_ref = place[1]
    for _ in range(3):
        line_ref = mark(line_ref)
    far_half = shift(half, "c", 1)
    inverse = chol_inverse(core_ref, half, far_half, orbs)
    out_type = jax.ShapeDtypeStruct((rows, orbs), jnp.float32)
    final_scratch = [pltpu.VMEM((rows, orbs), jnp.float32)]
    return call(final_kernel, out_type, final_scratch, {}, 10**9, 1, line_ref, *held, inverse)


def solution(mesh):
    fine = Mesh(mesh.devices.reshape(2, 8, 2, 2, 4), ("yl", "z", "c", "yh", "x"))
    blk = ("yl", "z", "c")

    return jax.shard_map(
        shards,
        mesh=fine,
        in_specs=(P(blk, None), P(None, blk)),
        out_specs=P(blk, None),
        check_vma=False,
    )
```

```python
import functools

import jax
import jax.numpy as jnp
from jax import lax
from jax.experimental import pallas as pl
from jax.experimental.pallas import tpu as pltpu
from jax.sharding import Mesh, PartitionSpec as P


HIGHEST = lax.Precision.HIGHEST
PLANE = ("x", "yh", "yl")

SIDE = 128


def lanes(value, index):
    return jnp.broadcast_to(value[:, index : index + 1], (8, SIDE))


def base(a_ref, z_ref, spread):
    strips = SIDE // 8
    lane = lax.broadcasted_iota(jnp.int32, (8, SIDE), 1)

    def opened(strip, block):
        start = 8 * strip
        inside = (lane >= start) & (lane < start + 8)
        for k in range(8):
            spread[8 * k : 8 * k + 8, :] = lanes(block, start + k)
        p = [[None] * 8 for _ in range(8)]
        for i in range(8):
            for k in range(i + 1):
                p[i][k] = p[k][i] = jnp.broadcast_to(spread[8 * k + i : 8 * k + i + 1, :], (8, SIDE))
        row = [jnp.broadcast_to(a_ref[start + i : start + i + 1, :], (8, SIDE)) for i in range(8)]
        row = [jnp.where(inside, jnp.where(lane == start + i, 1.0, 0.0), row[i]) for i in range(8)]
        return start, inside, row, p

    def update(strip, later, inside, row):
        there = slice(8 * later, 8 * later + 8)
        block = a_ref[there, :]
        product = [lanes(block, 8 * strip + k) * row[k] for k in range(8)]
        while len(product) > 1:
            product = [product[i] + product[i + 1] for i in range(0, len(product), 2)]
        block = jnp.where(inside, 0.0, block) - product[0]
        a_ref[there, :] = block
        return block

    state = opened(0, a_ref[:8, :])
    for strip in range(strips):
        start, inside, row, p = state
        for k in range(8):
            inv = 1.0 / p[k][k]
            z_ref[start + k : start + k + 1, :] = (row[k] * lax.rsqrt(p[k][k]))[:1]
            scaled = [None if i == k else p[i][k] * inv for i in range(8)]
            for i in list(range(k + 1, 8)) + list(range(k)):
                for l in range(k + 1, 8):
                    if i > k and l > i:
                        continue
                    if i == l == k + 1:
                        p[i][l] = p[i][l] - (p[i][k] * p[k][l]) * inv
                    else:
                        p[i][l] = p[i][l] - scaled[i] * p[k][l]
                    if i > k:
                        p[l][i] = p[i][l]
            for l in range(k + 1, 8):
                p[k][l] = scaled[l] if l > k else p[k][l]
            for i in range(8):
                if i != k:
                    row[i] = row[i] - scaled[i] * row[k]
            row[k] = row[k] * inv
        if strip + 1 < strips:
            state = opened(strip + 1, update(strip, strip + 1, inside, row))
        for later in range(strip + 2, strips):
            update(strip, later, inside, row)


def dot(a, b, dims, precision=HIGHEST):
    return lax.dot_general(a, b, (dims, ((), ())), precision=precision, preferred_element_type=jnp.float32)


def split(value):
    upper = value.astype(jnp.bfloat16)
    return upper, (value - upper.astype(jnp.float32)).astype(jnp.bfloat16)


def chol_kernel(core_ref, mine_ref, other_ref, z_ref, rows, base_a, base_z, spread):
    n = z_ref.shape[0]
    count = n // SIDE
    where = [(i, j) for i in range(count) for j in range(i, count)]
    each = len(where) // 2
    for number, (i, j) in enumerate(where):
        here = slice(number % each * SIDE, number % each * SIDE + SIDE)
        block = jnp.where(core_ref[0] == number // each, mine_ref[here, :], other_ref[here, :])
        z_ref[i * SIDE : i * SIDE + SIDE, j * SIDE : j * SIDE + SIDE] = block
        if i < j:
            z_ref[j * SIDE : j * SIDE + SIDE, i * SIDE : i * SIDE + SIDE] = jnp.zeros((SIDE, SIDE), jnp.float32)
    row = lax.broadcasted_iota(jnp.int32, (SIDE, SIDE), 0)
    column = lax.broadcasted_iota(jnp.int32, (SIDE, SIDE), 1)
    eye = jnp.where(row == column, 1.0, 0.0)

    def step(index, carry):
        here = pl.ds(pl.multiple_of(index * SIDE, SIDE), SIDE)
        base_a[...] = z_ref[here, here]
        base(base_a, base_z, spread)
        z_ref[here, here] = eye
        lower = jnp.where(row >= column, base_z[...], 0.0)
        rows[...] = dot(lower, z_ref[here, :], ((1,), (0,)))
        z_ref[here, :] = rows[...]

        def update(later, inner):
            there = pl.ds(pl.multiple_of(later * SIDE, SIDE), SIDE)
            z_ref[there, here] = jnp.zeros((SIDE, SIDE), jnp.float32)
            z_ref[there, :] = z_ref[there, :] - dot(rows[:, there], rows[...], ((0,), (0,)))
            return inner

        lax.fori_loop(index + 1, count, update, 0)
        return carry

    lax.fori_loop(0, count, step, 0)
    for i in range(count):
        for j in range(i + 1, count):
            z_ref[i * SIDE : i * SIDE + SIDE, j * SIDE : j * SIDE + SIDE] = jnp.zeros((SIDE, SIDE), jnp.float32)


def call(body, out_shape, scratch, aliases, flops, scalars, *operands):
    vmem = pl.BlockSpec(memory_space=pltpu.VMEM)
    smem = pl.BlockSpec(memory_space=pltpu.SMEM)
    return pl.pallas_call(
        body,
        out_shape=out_shape,
        in_specs=[smem] * scalars + [vmem] * (len(operands) - scalars),
        out_specs=jax.tree.map(lambda _: vmem, out_shape),
        scratch_shapes=scratch,
        input_output_aliases=aliases,
        cost_estimate=pl.CostEstimate(flops=flops, transcendentals=0, bytes_accessed=2 * 10**6),
        compiler_params=pltpu.CompilerParams(vmem_limit_bytes=16 * 2**20),
    )(*operands)


def chol_inverse(core, mine, other, n):
    scratch = [pltpu.VMEM(s, jnp.float32) for s in ((SIDE, n), (SIDE, SIDE), (SIDE, SIDE), (64, SIDE))]
    return call(chol_kernel, jax.ShapeDtypeStruct((n, n), jnp.float32), scratch, {}, 2 * 10**10, 1, core, mine, other)


def near_kernel(lower_ref, upper_ref, below_ref, above_ref, near_ref, turned_ref, spread_ref):
    middle, orbs = lower_ref.shape[0] - 8, lower_ref.shape[1]
    tall = near_ref.shape[0]
    for part, ref in enumerate((lower_ref, upper_ref, below_ref, above_ref)):
        there = slice(part * middle, part * middle + middle)
        value = ref[:middle, :]
        upper, lower = split(value)
        near_ref[there, :orbs] = upper
        near_ref[there, orbs : 2 * orbs] = upper
        near_ref[there, 2 * orbs :] = lower
        upper, lower = split(value.T)
        for place, half in enumerate((upper, upper, lower)):
            turned_ref[:, place * tall + part * middle : place * tall + part * middle + middle] = half
        for k in range(3):
            line = ref[middle + k : middle + k + 1, :middle]
            spread_ref[k, there, :] = jnp.broadcast_to(line, (SIDE, middle)).T


def add_tile(near_ref, spread_ref, acc, out, pieces, wide_far, tall_far, slab):
    chunk = pieces[0].shape[0] - 8
    orbs = out.shape[1]
    width = len(pieces) * chunk
    lane = lax.broadcasted_iota(jnp.int32, (8, SIDE), 1)
    for number, piece in enumerate(pieces):
        upper, lower = split(piece[:chunk, :])
        here = slice(number * chunk, number * chunk + chunk)
        for place, half in enumerate((upper, lower, upper)):
            wide_far[here, place * orbs : place * orbs + orbs] = half
            tall_far[place * width + number * chunk : place * width + number * chunk + chunk, :] = half
    for number in range(0, len(pieces), 2):
        left, right = (pieces[number + i][chunk : chunk + 8, :SIDE] for i in range(2))
        at = number * chunk
        slab[:, at : at + SIDE] = jnp.where(lane < chunk, left, pltpu.roll(right, chunk, 1))
    step = out.shape[0]
    for index in range(out.shape[0] // step):
        here = slice(index * step, index * step + step)
        gram = dot(near_ref[here, :], wide_far[...], ((1,), (1,)), None)
        squares = []
        for at in range(0, width, SIDE):
            square = 0.0025
            for k in range(3):
                spacing = spread_ref[k, here, :] - slab[k : k + 1, at : at + SIDE]
                square = square + spacing * spacing
            squares.append(square)
        upper, lower = split(gram * lax.rsqrt(jnp.concatenate(squares, axis=1)))
        product = dot(jnp.concatenate([upper, upper, lower], axis=1), tall_far[...], ((1,), (0,)), None)
        out[here, :] = product if acc is None else acc[here, :] + product


def first_kernel(pieces, *refs):
    found, out, scratch = refs[2 : 2 + pieces], refs[2 + pieces], refs[3 + pieces :]
    add_tile(*refs[:2], None, out, found, *scratch)


def tile_kernel(pieces, *refs):
    acc, found, out, scratch = refs[2], refs[3 : 3 + pieces], refs[3 + pieces], refs[4 + pieces :]
    add_tile(*refs[:2], acc, out, found, *scratch)


def last_kernel(pieces, weight, core_ref, near_ref, spread_ref, turned_ref, acc, *refs):
    found = refs[:pieces]
    own_ref, below_ref, above_ref, mine_ref, other_ref, total, halves = refs[pieces : 7 + pieces]
    add_tile(near_ref, spread_ref, acc, total, found, *refs[7 + pieces :])
    rows = own_ref.shape[0]
    middle = rows // 2
    tall = 2 * rows
    own_ref[...] = total[:rows, :] * weight
    below_ref[...] = total[rows : rows + middle, :] * weight
    above_ref[...] = total[rows + middle :, :] * weight
    upper, lower = split(total[...])
    for place, half in enumerate((upper, lower, upper)):
        halves[place * tall : place * tall + tall, :] = half
    count = total.shape[1] // SIDE
    number = 0
    each = count * (count + 1) // 4
    square = dot(turned_ref[...], halves[...], ((1,), (0,)), None) * (weight * weight)
    for i in range(count):
        for j in range(i, count):
            block = square[i * SIDE : i * SIDE + SIDE, j * SIDE : j * SIDE + SIDE]
            there = slice(number % each * SIDE, number % each * SIDE + SIDE)

            @pl.when(core_ref[0] == number // each)
            def _():
                mine_ref[there, :] = block

            @pl.when(core_ref[0] != number // each)
            def _():
                other_ref[there, :] = block

            number += 1


def pack_kernel(group_ref, core_ref, line_ref, rows_ref, points_ref, own_ref, below_ref, above_ref):
    chunk = own_ref.shape[0] - 8
    rows, orbs = rows_ref.shape
    middle = rows // 2
    own_ref[:chunk, :] = rows_ref[pl.ds(pl.multiple_of(group_ref[0] * chunk, chunk), chunk), :]
    for line in range(3):
        turned = pltpu.roll(jnp.broadcast_to(points_ref[line : line + 1, :], (8, rows)), rows - group_ref[0] * chunk, 1)
        own_ref[chunk + line : chunk + line + 1, :] = turned[:1, :orbs]
    own_ref[chunk + 3 :, :] = jnp.zeros((5, orbs), jnp.float32)
    for start, ref in ((0, below_ref), (middle, above_ref)):
        ref[:middle, :] = rows_ref[start : start + middle, :]
        ref[middle:, :] = jnp.zeros((8, orbs), jnp.float32)
        ref[middle : middle + 3, :middle] = points_ref[:, start : start + middle]


def mark_kernel(number_ref, out_ref):
    out_ref[0] = number_ref[0]


def mark(number):
    smem = pl.BlockSpec(memory_space=pltpu.SMEM)
    out_shape = jax.ShapeDtypeStruct((1,), jnp.int32)
    params = pltpu.CompilerParams(vmem_limit_bytes=2**20)
    return pl.pallas_call(mark_kernel, out_shape=out_shape, in_specs=[smem], out_specs=smem, compiler_params=params)(number)


def final_kernel(line_ref, *refs):
    pieces, inverse_ref, out_ref, joined = refs[:-3], refs[-3], refs[-2], refs[-1]
    lines, halves, chunk = len(pieces), pieces[0].shape[0], pieces[0].shape[1]
    for number, piece in enumerate(pieces):
        for half in range(halves):
            at = (number * halves + half) * chunk
            joined[at : at + chunk, :] = piece[half]

    def block(pair, carry):
        start = pl.multiple_of(pair * 2 * halves * chunk, 2 * halves * chunk)
        product = dot(joined[pl.ds(start, 2 * halves * chunk), :], inverse_ref[...], ((1,), (1,)))
        for step in range(2):
            sender = (line_ref[0] + (lines - 2 * pair - step)) % lines
            for half in range(halves):
                at = (step * halves + half) * chunk
                there = pl.ds(pl.multiple_of((half * lines + sender) * chunk, chunk), chunk)
                out_ref[there, :] = -product[at : at + chunk, :]
        return carry

    lax.fori_loop(0, lines // 2, block, 0)


def mix_kernel(line_ref, own_ref, above_ref, below_ref, *parts):
    lines, chunk = len(parts), parts[0].shape[1]
    for distance, part in enumerate(parts):
        target = (line_ref[0] + distance) % lines
        there = pl.ds(pl.multiple_of(target * chunk, chunk), chunk)
        behind = pl.ds(pl.multiple_of((lines + target) * chunk, chunk), chunk)
        part[0] = own_ref[there, :] + above_ref[there, :]
        part[1] = own_ref[behind, :] + below_ref[there, :]


def pick_kernel(core_ref, zero_ref, one_ref, out_ref):
    out_ref[...] = jnp.where(core_ref[0] == 0, zero_ref[...], one_ref[...])


def copies_kernel(parts_ref, out_ref):
    total = parts_ref[0]
    for number in range(1, parts_ref.shape[0]):
        total = total + parts_ref[number]
    for number in range(out_ref.shape[0]):
        out_ref[number] = total


def scratch(pieces, chunk, orbs):
    wide = pieces * chunk
    return [
        pltpu.VMEM((wide, 3 * orbs), jnp.bfloat16),
        pltpu.VMEM((3 * wide, orbs), jnp.bfloat16),
        pltpu.VMEM((8, wide), jnp.float32),
    ]


def shift(block, axis, distance):
    size = lax.axis_size(axis)
    return lax.ppermute(block, axis, [(i, (i + distance) % size) for i in range(size)])


def shift_y(block, distance):
    size = lax.axis_size(("yl", "yh"))
    place = [(y % 2) * (size // 2) + y // 2 for y in range(size)]
    return lax.ppermute(block, ("yl", "yh"), [(place[y], place[(y + distance) % size]) for y in range(size)])


def exchanged(parts, axes):
    return lax.all_to_all(parts, axes, 0, 0, tiled=True)


def summed_copies(parts, copies):
    return call(copies_kernel, jax.ShapeDtypeStruct((copies,) + parts.shape[1:], parts.dtype), [], {}, 10**6, 0, parts)


def shards(orbitals, points):
    rows, orbs = orbitals.shape
    core = lax.axis_index("c")
    line = lax.axis_index("x")
    core_ref = core.astype(jnp.int32)[None]
    place = [core_ref, line.astype(jnp.int32)[None]]
    groups = lax.axis_size(("yh", "x"))
    group = lax.axis_index(("yh", "x"))
    chunk = rows // groups
    weight = 1.0 / (rows * lax.axis_size(("yl", "z", "c")))

    middle = rows // 2
    message = [jax.ShapeDtypeStruct((size + 8, orbs), jnp.float32) for size in (chunk, middle, middle)]
    group_ref = group.astype(jnp.int32)[None]
    own, lower_half, upper_half = call(pack_kernel, tuple(message), [], {}, 10**8, 3, group_ref, *place, orbitals, points)
    from_below = shift_y(lower_half, 1)
    from_above = shift_y(upper_half, -1)
    far = {0: own}
    ring = lax.axis_size("z")
    order = [0]
    for distance in range(1, ring // 2):
        order += [distance, -distance]
    order.append(ring // 2)
    for distance in order[1:-1]:
        far[distance] = shift(own, "z", distance)
    relay = [(2 * z + c, 2 * ((z + 1 - 2 * c) % ring) + c) for z in range(ring) for c in range(2)]
    carried = call(pick_kernel, message[0], [], {}, 10**6, 1, core_ref, far[ring // 2 - 1], far[1 - ring // 2])
    far[ring // 2] = lax.ppermute(carried, ("z", "c"), relay)

    tall = 2 * rows
    near_type = jax.ShapeDtypeStruct((tall, 3 * orbs), jnp.bfloat16)
    turned_type = jax.ShapeDtypeStruct((orbs, 3 * tall), jnp.bfloat16)
    spread_type = jax.ShapeDtypeStruct((3, tall, SIDE), jnp.float32)
    near, turned, spread = call(
        near_kernel, (near_type, turned_type, spread_type), [], {}, 10**9, 0, lower_half, upper_half, from_below, from_above
    )
    total_type = jax.ShapeDtypeStruct((tall, orbs), jnp.float32)
    stages = [order[:3], order[3:5], order[5:7], order[7:]]
    total = None
    for number, stage in enumerate(stages):
        pieces = []
        for distance in stage:
            pieces += [far[distance], shift(far[distance], "c", 1)]
        count = len(pieces)
        if number == 0:
            body = functools.partial(first_kernel, count)
            total = call(body, total_type, scratch(count, chunk, orbs), {}, 4 * 10**9, 0, near, spread, *pieces)
        elif number < len(stages) - 1:
            body = functools.partial(tile_kernel, count)
            total = call(body, total_type, scratch(count, chunk, orbs), {2: 0}, 3 * 10**9, 0, near, spread, total, *pieces)
    tri = (orbs // SIDE) * (orbs // SIDE + 1) // 4 * SIDE
    middle_type = jax.ShapeDtypeStruct((middle, orbs), jnp.float32)
    tri_type = jax.ShapeDtypeStruct((tri, SIDE), jnp.float32)
    own_part, to_above, to_below, mine, other = call(
        functools.partial(last_kernel, count, weight),
        (jax.ShapeDtypeStruct((rows, orbs), jnp.float32), middle_type, middle_type, tri_type, tri_type),
        [pltpu.VMEM((tall, orbs), jnp.float32), pltpu.VMEM((3 * tall, orbs), jnp.bfloat16)] + scratch(count, chunk, orbs),
        {}, 3 * 10**9, 1, core_ref, near, spread, turned, total, *pieces,
    )

    half = mine + shift(other, "c", 1)
    to_above = shift_y(to_above, 1)
    to_below = shift_y(to_below, -1)
    plane = lax.axis_size(PLANE)
    pieces = exchanged(half.reshape(plane, -1, SIDE), PLANE)
    pieces = summed_copies(pieces, ring)
    pieces = exchanged(pieces, "z")
    lines = lax.axis_size("x")
    part_type = jax.ShapeDtypeStruct((groups // lines, chunk, orbs), jnp.float32)
    parts = call(mix_kernel, (part_type,) * lines, [], {}, 10**8, 1, place[1], own_part, to_above, to_below)
    held = [parts[0]]
    for distance in range(1, lines):
        held.append(shift(parts[distance], "x", distance))
    pieces = summed_copies(pieces, plane)
    half = exchanged(pieces, PLANE).reshape(-1, SIDE)
    pair = sum(held[1:], held[0])
    other_pair = shift(pair, "yh", 1)
    pair = pair + other_pair
    held = [pair]
    for distance in range(1, lines):
        held.append(shift(pair, "x", distance))
    line_ref = place[1]
    for _ in range(2):
        line_ref = mark(line_ref)
    far_half = shift(half, "c", 1)
    inverse = chol_inverse(core_ref, half, far_half, orbs)
    out_type = jax.ShapeDtypeStruct((rows, orbs), jnp.float32)
    final_scratch = [pltpu.VMEM((rows, orbs), jnp.float32)]
    return call(final_kernel, out_type, final_scratch, {}, 10**9, 1, line_ref, *held, inverse)


def solution(mesh):
    fine = Mesh(mesh.devices.reshape(2, 8, 2, 2, 4), ("yl", "z", "c", "yh", "x"))
    blk = ("yl", "z", "c")

    return jax.shard_map(
        shards,
        mesh=fine,
        in_specs=(P(blk, None), P(None, blk)),
        out_specs=P(blk, None),
        check_vma=False,
    )
```

```python
import functools

import jax
import jax.numpy as jnp
from jax import lax
from jax.experimental import pallas as pl
from jax.experimental.pallas import tpu as pltpu
from jax.sharding import Mesh, PartitionSpec as P


HIGHEST = lax.Precision.HIGHEST
PLANE = ("x", "yh", "yl")

SIDE = 128


def lanes(value, index):
    return jnp.broadcast_to(value[:, index : index + 1], (8, SIDE))


def base(a_ref, z_ref, spread):
    strips = SIDE // 8
    lane = lax.broadcasted_iota(jnp.int32, (8, SIDE), 1)

    def opened(strip, block):
        start = 8 * strip
        inside = (lane >= start) & (lane < start + 8)
        for k in range(8):
            spread[8 * k : 8 * k + 8, :] = lanes(block, start + k)
        p = [[None] * 8 for _ in range(8)]
        for i in range(8):
            for k in range(i + 1):
                p[i][k] = p[k][i] = jnp.broadcast_to(spread[8 * k + i : 8 * k + i + 1, :], (8, SIDE))
        row = [jnp.broadcast_to(a_ref[start + i : start + i + 1, :], (8, SIDE)) for i in range(8)]
        row = [jnp.where(inside, jnp.where(lane == start + i, 1.0, 0.0), row[i]) for i in range(8)]
        return start, inside, row, p

    def update(strip, later, inside, row):
        there = slice(8 * later, 8 * later + 8)
        block = a_ref[there, :]
        product = [lanes(block, 8 * strip + k) * row[k] for k in range(8)]
        while len(product) > 1:
            product = [product[i] + product[i + 1] for i in range(0, len(product), 2)]
        block = jnp.where(inside, 0.0, block) - product[0]
        a_ref[there, :] = block
        return block

    state = opened(0, a_ref[:8, :])
    for strip in range(strips):
        start, inside, row, p = state
        for k in range(8):
            inv = 1.0 / p[k][k]
            z_ref[start + k : start + k + 1, :] = (row[k] * lax.rsqrt(p[k][k]))[:1]
            scaled = [None if i == k else p[i][k] * inv for i in range(8)]
            for i in list(range(k + 1, 8)) + list(range(k)):
                for l in range(k + 1, 8):
                    if i > k and l > i:
                        continue
                    if i == l == k + 1:
                        p[i][l] = p[i][l] - (p[i][k] * p[k][l]) * inv
                    else:
                        p[i][l] = p[i][l] - scaled[i] * p[k][l]
                    if i > k:
                        p[l][i] = p[i][l]
            for l in range(k + 1, 8):
                p[k][l] = scaled[l] if l > k else p[k][l]
            for i in range(8):
                if i != k:
                    row[i] = row[i] - scaled[i] * row[k]
            row[k] = row[k] * inv
        if strip + 1 < strips:
            state = opened(strip + 1, update(strip, strip + 1, inside, row))
        for later in range(strip + 2, strips):
            update(strip, later, inside, row)


def dot(a, b, dims, precision=HIGHEST):
    return lax.dot_general(a, b, (dims, ((), ())), precision=precision, preferred_element_type=jnp.float32)


def split(value):
    upper = value.astype(jnp.bfloat16)
    return upper, (value - upper.astype(jnp.float32)).astype(jnp.bfloat16)


def chol_kernel(core_ref, mine_ref, other_ref, z_ref, rows, base_a, base_z, spread):
    n = z_ref.shape[0]
    count = n // SIDE
    where = [(i, j) for i in range(count) for j in range(i, count)]
    each = len(where) // 2
    for number, (i, j) in enumerate(where):
        here = slice(number % each * SIDE, number % each * SIDE + SIDE)
        block = jnp.where(core_ref[0] == number // each, mine_ref[here, :], other_ref[here, :])
        z_ref[i * SIDE : i * SIDE + SIDE, j * SIDE : j * SIDE + SIDE] = block
        if i < j:
            z_ref[j * SIDE : j * SIDE + SIDE, i * SIDE : i * SIDE + SIDE] = jnp.zeros((SIDE, SIDE), jnp.float32)
    row = lax.broadcasted_iota(jnp.int32, (SIDE, SIDE), 0)
    column = lax.broadcasted_iota(jnp.int32, (SIDE, SIDE), 1)
    eye = jnp.where(row == column, 1.0, 0.0)

    def step(index, carry):
        here = pl.ds(pl.multiple_of(index * SIDE, SIDE), SIDE)
        base_a[...] = z_ref[here, here]
        base(base_a, base_z, spread)
        z_ref[here, here] = eye
        lower = jnp.where(row >= column, base_z[...], 0.0)
        rows[...] = dot(lower, z_ref[here, :], ((1,), (0,)))
        z_ref[here, :] = rows[...]

        def update(later, inner):
            there = pl.ds(pl.multiple_of(later * SIDE, SIDE), SIDE)
            z_ref[there, here] = jnp.zeros((SIDE, SIDE), jnp.float32)
            z_ref[there, :] = z_ref[there, :] - dot(rows[:, there], rows[...], ((0,), (0,)))
            return inner

        lax.fori_loop(index + 1, count, update, 0)
        return carry

    lax.fori_loop(0, count, step, 0)
    for i in range(count):
        for j in range(i + 1, count):
            z_ref[i * SIDE : i * SIDE + SIDE, j * SIDE : j * SIDE + SIDE] = jnp.zeros((SIDE, SIDE), jnp.float32)


def call(body, out_shape, scratch, aliases, flops, scalars, *operands):
    vmem = pl.BlockSpec(memory_space=pltpu.VMEM)
    smem = pl.BlockSpec(memory_space=pltpu.SMEM)
    return pl.pallas_call(
        body,
        out_shape=out_shape,
        in_specs=[smem] * scalars + [vmem] * (len(operands) - scalars),
        out_specs=jax.tree.map(lambda _: vmem, out_shape),
        scratch_shapes=scratch,
        input_output_aliases=aliases,
        cost_estimate=pl.CostEstimate(flops=flops, transcendentals=0, bytes_accessed=2 * 10**6),
        compiler_params=pltpu.CompilerParams(vmem_limit_bytes=16 * 2**20),
    )(*operands)


def chol_inverse(core, mine, other, n):
    scratch = [pltpu.VMEM(s, jnp.float32) for s in ((SIDE, n), (SIDE, SIDE), (SIDE, SIDE), (64, SIDE))]
    return call(chol_kernel, jax.ShapeDtypeStruct((n, n), jnp.float32), scratch, {}, 2 * 10**10, 1, core, mine, other)


def near_kernel(lower_ref, upper_ref, below_ref, above_ref, near_ref, turned_ref, spread_ref):
    middle, orbs = lower_ref.shape[0] - 8, lower_ref.shape[1]
    tall = near_ref.shape[0]
    for part, ref in enumerate((lower_ref, upper_ref, below_ref, above_ref)):
        there = slice(part * middle, part * middle + middle)
        value = ref[:middle, :]
        upper, lower = split(value)
        near_ref[there, :orbs] = upper
        near_ref[there, orbs : 2 * orbs] = upper
        near_ref[there, 2 * orbs :] = lower
        upper, lower = split(value.T)
        for place, half in enumerate((upper, upper, lower)):
            turned_ref[:, place * tall + part * middle : place * tall + part * middle + middle] = half
        for k in range(3):
            line = ref[middle + k : middle + k + 1, :middle]
            spread_ref[k, there, :] = jnp.broadcast_to(line, (SIDE, middle)).T


def add_tile(near_ref, spread_ref, acc, out, pieces, wide_far, tall_far, slab):
    chunk = pieces[0].shape[0] - 8
    orbs = out.shape[1]
    width = len(pieces) * chunk
    lane = lax.broadcasted_iota(jnp.int32, (8, SIDE), 1)
    for number, piece in enumerate(pieces):
        upper, lower = split(piece[:chunk, :])
        here = slice(number * chunk, number * chunk + chunk)
        for place, half in enumerate((upper, lower, upper)):
            wide_far[here, place * orbs : place * orbs + orbs] = half
            tall_far[place * width + number * chunk : place * width + number * chunk + chunk, :] = half
    for number in range(0, len(pieces), 2):
        left, right = (pieces[number + i][chunk : chunk + 8, :SIDE] for i in range(2))
        at = number * chunk
        slab[:, at : at + SIDE] = jnp.where(lane < chunk, left, pltpu.roll(right, chunk, 1))
    step = out.shape[0]
    for index in range(out.shape[0] // step):
        here = slice(index * step, index * step + step)
        gram = dot(near_ref[here, :], wide_far[...], ((1,), (1,)), None)
        squares = []
        for at in range(0, width, SIDE):
            square = 0.0025
            for k in range(3):
                spacing = spread_ref[k, here, :] - slab[k : k + 1, at : at + SIDE]
                square = square + spacing * spacing
            squares.append(square)
        upper, lower = split(gram * lax.rsqrt(jnp.concatenate(squares, axis=1)))
        product = dot(jnp.concatenate([upper, upper, lower], axis=1), tall_far[...], ((1,), (0,)), None)
        out[here, :] = product if acc is None else acc[here, :] + product


def first_kernel(pieces, *refs):
    found, out, scratch = refs[2 : 2 + pieces], refs[2 + pieces], refs[3 + pieces :]
    add_tile(*refs[:2], None, out, found, *scratch)


def tile_kernel(pieces, *refs):
    acc, found, out, scratch = refs[2], refs[3 : 3 + pieces], refs[3 + pieces], refs[4 + pieces :]
    add_tile(*refs[:2], acc, out, found, *scratch)


def last_kernel(pieces, weight, core_ref, near_ref, spread_ref, turned_ref, acc, *refs):
    found = refs[:pieces]
    own_ref, below_ref, above_ref, mine_ref, other_ref, total, halves = refs[pieces : 7 + pieces]
    add_tile(near_ref, spread_ref, acc, total, found, *refs[7 + pieces :])
    rows = own_ref.shape[0]
    middle = rows // 2
    tall = 2 * rows
    own_ref[...] = total[:rows, :] * weight
    below_ref[...] = total[rows : rows + middle, :] * weight
    above_ref[...] = total[rows + middle :, :] * weight
    upper, lower = split(total[...])
    for place, half in enumerate((upper, lower, upper)):
        halves[place * tall : place * tall + tall, :] = half
    count = total.shape[1] // SIDE
    number = 0
    each = count * (count + 1) // 4
    square = dot(turned_ref[...], halves[...], ((1,), (0,)), None) * (weight * weight)
    for i in range(count):
        for j in range(i, count):
            block = square[i * SIDE : i * SIDE + SIDE, j * SIDE : j * SIDE + SIDE]
            there = slice(number % each * SIDE, number % each * SIDE + SIDE)

            @pl.when(core_ref[0] == number // each)
            def _():
                mine_ref[there, :] = block

            @pl.when(core_ref[0] != number // each)
            def _():
                other_ref[there, :] = block

            number += 1


def pack_kernel(group_ref, core_ref, line_ref, rows_ref, points_ref, own_ref, below_ref, above_ref):
    chunk = own_ref.shape[0] - 8
    rows, orbs = rows_ref.shape
    middle = rows // 2
    own_ref[:chunk, :] = rows_ref[pl.ds(pl.multiple_of(group_ref[0] * chunk, chunk), chunk), :]
    for line in range(3):
        turned = pltpu.roll(jnp.broadcast_to(points_ref[line : line + 1, :], (8, rows)), rows - group_ref[0] * chunk, 1)
        own_ref[chunk + line : chunk + line + 1, :] = turned[:1, :orbs]
    own_ref[chunk + 3 :, :] = jnp.zeros((5, orbs), jnp.float32)
    for start, ref in ((0, below_ref), (middle, above_ref)):
        ref[:middle, :] = rows_ref[start : start + middle, :]
        ref[middle:, :] = jnp.zeros((8, orbs), jnp.float32)
        ref[middle : middle + 3, :middle] = points_ref[:, start : start + middle]


def mark_kernel(number_ref, out_ref):
    out_ref[0] = number_ref[0]


def mark(number):
    smem = pl.BlockSpec(memory_space=pltpu.SMEM)
    out_shape = jax.ShapeDtypeStruct((1,), jnp.int32)
    params = pltpu.CompilerParams(vmem_limit_bytes=2**20)
    return pl.pallas_call(mark_kernel, out_shape=out_shape, in_specs=[smem], out_specs=smem, compiler_params=params)(number)


def final_kernel(line_ref, *refs):
    pieces, inverse_ref, out_ref, joined = refs[:-3], refs[-3], refs[-2], refs[-1]
    lines, halves, chunk = len(pieces), pieces[0].shape[0], pieces[0].shape[1]
    for number, piece in enumerate(pieces):
        for half in range(halves):
            at = (number * halves + half) * chunk
            joined[at : at + chunk, :] = piece[half]

    product = dot(joined[...], inverse_ref[...], ((1,), (1,)))
    for number in range(lines):
        sender = (line_ref[0] + (lines - number)) % lines
        for half in range(halves):
            at = (number * halves + half) * chunk
            there = pl.ds(pl.multiple_of((half * lines + sender) * chunk, chunk), chunk)
            out_ref[there, :] = -product[at : at + chunk, :]


def mix_kernel(line_ref, own_ref, above_ref, below_ref, *parts):
    lines, chunk = len(parts), parts[0].shape[1]
    for distance, part in enumerate(parts):
        target = (line_ref[0] + distance) % lines
        there = pl.ds(pl.multiple_of(target * chunk, chunk), chunk)
        behind = pl.ds(pl.multiple_of((lines + target) * chunk, chunk), chunk)
        part[0] = own_ref[there, :] + above_ref[there, :]
        part[1] = own_ref[behind, :] + below_ref[there, :]


def pick_kernel(core_ref, zero_ref, one_ref, out_ref):
    out_ref[...] = jnp.where(core_ref[0] == 0, zero_ref[...], one_ref[...])


def copies_kernel(parts_ref, out_ref):
    total = parts_ref[0]
    for number in range(1, parts_ref.shape[0]):
        total = total + parts_ref[number]
    for number in range(out_ref.shape[0]):
        out_ref[number] = total


def scratch(pieces, chunk, orbs):
    wide = pieces * chunk
    return [
        pltpu.VMEM((wide, 3 * orbs), jnp.bfloat16),
        pltpu.VMEM((3 * wide, orbs), jnp.bfloat16),
        pltpu.VMEM((8, wide), jnp.float32),
    ]


def shift(block, axis, distance):
    size = lax.axis_size(axis)
    return lax.ppermute(block, axis, [(i, (i + distance) % size) for i in range(size)])


def shift_y(block, distance):
    size = lax.axis_size(("yl", "yh"))
    place = [(y % 2) * (size // 2) + y // 2 for y in range(size)]
    return lax.ppermute(block, ("yl", "yh"), [(place[y], place[(y + distance) % size]) for y in range(size)])


def exchanged(parts, axes):
    return lax.all_to_all(parts, axes, 0, 0, tiled=True)


def summed_copies(parts, copies):
    return call(copies_kernel, jax.ShapeDtypeStruct((copies,) + parts.shape[1:], parts.dtype), [], {}, 10**6, 0, parts)


def shards(orbitals, points):
    rows, orbs = orbitals.shape
    core = lax.axis_index("c")
    line = lax.axis_index("x")
    core_ref = core.astype(jnp.int32)[None]
    place = [core_ref, line.astype(jnp.int32)[None]]
    groups = lax.axis_size(("yh", "x"))
    group = lax.axis_index(("yh", "x"))
    chunk = rows // groups
    weight = 1.0 / (rows * lax.axis_size(("yl", "z", "c")))

    middle = rows // 2
    message = [jax.ShapeDtypeStruct((size + 8, orbs), jnp.float32) for size in (chunk, middle, middle)]
    group_ref = group.astype(jnp.int32)[None]
    own, lower_half, upper_half = call(pack_kernel, tuple(message), [], {}, 10**8, 3, group_ref, *place, orbitals, points)
    from_below = shift_y(lower_half, 1)
    from_above = shift_y(upper_half, -1)
    far = {0: own}
    ring = lax.axis_size("z")
    order = [0]
    for distance in range(1, ring // 2):
        order += [distance, -distance]
    order.append(ring // 2)
    for distance in order[1:-1]:
        far[distance] = shift(own, "z", distance)
    relay = [(2 * z + c, 2 * ((z + 1 - 2 * c) % ring) + c) for z in range(ring) for c in range(2)]
    carried = call(pick_kernel, message[0], [], {}, 10**6, 1, core_ref, far[ring // 2 - 1], far[1 - ring // 2])
    far[ring // 2] = lax.ppermute(carried, ("z", "c"), relay)

    tall = 2 * rows
    near_type = jax.ShapeDtypeStruct((tall, 3 * orbs), jnp.bfloat16)
    turned_type = jax.ShapeDtypeStruct((orbs, 3 * tall), jnp.bfloat16)
    spread_type = jax.ShapeDtypeStruct((3, tall, SIDE), jnp.float32)
    near, turned, spread = call(
        near_kernel, (near_type, turned_type, spread_type), [], {}, 10**9, 0, lower_half, upper_half, from_below, from_above
    )
    total_type = jax.ShapeDtypeStruct((tall, orbs), jnp.float32)
    stages = [order[:3], order[3:5], order[5:7], order[7:]]
    total = None
    for number, stage in enumerate(stages):
        pieces = []
        for distance in stage:
            pieces += [far[distance], shift(far[distance], "c", 1)]
        count = len(pieces)
        if number == 0:
            body = functools.partial(first_kernel, count)
            total = call(body, total_type, scratch(count, chunk, orbs), {}, 4 * 10**9, 0, near, spread, *pieces)
        elif number < len(stages) - 1:
            body = functools.partial(tile_kernel, count)
            total = call(body, total_type, scratch(count, chunk, orbs), {2: 0}, 3 * 10**9, 0, near, spread, total, *pieces)
    tri = (orbs // SIDE) * (orbs // SIDE + 1) // 4 * SIDE
    middle_type = jax.ShapeDtypeStruct((middle, orbs), jnp.float32)
    tri_type = jax.ShapeDtypeStruct((tri, SIDE), jnp.float32)
    own_part, to_above, to_below, mine, other = call(
        functools.partial(last_kernel, count, weight),
        (jax.ShapeDtypeStruct((rows, orbs), jnp.float32), middle_type, middle_type, tri_type, tri_type),
        [pltpu.VMEM((tall, orbs), jnp.float32), pltpu.VMEM((3 * tall, orbs), jnp.bfloat16)] + scratch(count, chunk, orbs),
        {}, 3 * 10**9, 1, core_ref, near, spread, turned, total, *pieces,
    )

    half = mine + shift(other, "c", 1)
    to_above = shift_y(to_above, 1)
    to_below = shift_y(to_below, -1)
    plane = lax.axis_size(PLANE)
    pieces = exchanged(half.reshape(plane, -1, SIDE), PLANE)
    pieces = summed_copies(pieces, ring)
    pieces = exchanged(pieces, "z")
    lines = lax.axis_size("x")
    part_type = jax.ShapeDtypeStruct((groups // lines, chunk, orbs), jnp.float32)
    parts = call(mix_kernel, (part_type,) * lines, [], {}, 10**8, 1, place[1], own_part, to_above, to_below)
    held = [parts[0]]
    for distance in range(1, lines):
        held.append(shift(parts[distance], "x", distance))
    pieces = summed_copies(pieces, plane)
    half = exchanged(pieces, PLANE).reshape(-1, SIDE)
    pair = sum(held[1:], held[0])
    other_pair = shift(pair, "yh", 1)
    pair = pair + other_pair
    held = [pair]
    for distance in range(1, lines):
        held.append(shift(pair, "x", distance))
    line_ref = place[1]
    for _ in range(2):
        line_ref = mark(line_ref)
    far_half = shift(half, "c", 1)
    inverse = chol_inverse(core_ref, half, far_half, orbs)
    out_type = jax.ShapeDtypeStruct((rows, orbs), jnp.float32)
    final_scratch = [pltpu.VMEM((rows, orbs), jnp.float32)]
    return call(final_kernel, out_type, final_scratch, {}, 10**9, 1, line_ref, *held, inverse)


def solution(mesh):
    fine = Mesh(mesh.devices.reshape(2, 8, 2, 2, 4), ("yl", "z", "c", "yh", "x"))
    blk = ("yl", "z", "c")

    return jax.shard_map(
        shards,
        mesh=fine,
        in_specs=(P(blk, None), P(None, blk)),
        out_specs=P(blk, None),
        check_vma=False,
    )
```
